128 devices in a mesh: emb: 32 (over z, y, core), seq: 4 (over x).
Axes of the slice: x: 4, y: 4, z: 4, core: 2. Of those that a mesh axis runs over, the one named last changes fastest.
Arguments:
- item_table: bfloat16 [131072, 512], P(('emb', 'seq')), may hold values from -6 to 6
- unique_ids: int32 [32768], P(('emb', 'seq')), may hold values from 0 to 131071, as said below
- inverse: int32 [1024, 256], P(('emb', 'seq')), may hold values from 0 to 255, as said below
- lengths: int32 [1024], P(('emb', 'seq')), may hold values from 64 to 256, as said below
- assignment: int32 [1024], P(('emb', 'seq')), may hold values from 0 to 31, as said below
- proj_in: bfloat16 [512, 2048], replicated, may hold values from -0.25 to 0.25
- bias_in: float32 [2048], replicated, may hold values from -3 to 3
- gain_in: float32 [512], replicated, may hold values from 0.1 to 1.9
- gain_mid: float32 [512], replicated, may hold values from 0.1 to 1.9
- proj_out: bfloat16 [512, 512], replicated, may hold values from -0.25 to 0.25
- position_bias: float32 [4, 256], replicated, may hold values from -4 to 4
- cotangent: bfloat16 [1024, 256, 512], P(('emb', 'seq')), may hold values from -6 to 6
Outputs:
- outputs: bfloat16 [1024, 256, 512], P(('emb', 'seq'))
- table_grad: float32 [131072, 512], P(('emb', 'seq'))
The draws below stay inside these ranges and needn't reach their ends.
Inputs may be any that keep to these rules, and one draw needn't show every extreme that they name: `unique_ids`: each device's 256 entries are distinct row numbers; row r is held by device r // 1024; a device names at most 4 rows held by any one device, and exactly 4 of some device. `inverse`: every entry of a device's unique list is named by some token at a position below its slot's length. `lengths`: every group of 4 devices along seq has a slot of length 256. `assignment`: value v of a slot of a device with emb index e places it in slot v % 8 of the device with emb index e and seq index v // 8. Within a group it is a permutation, and the slots that the device with seq index s sends to a device take that device's slots s * 2 to (s + 1) * 2 - 1.
All inputs are finite; a program needn't handle non-finite values.
Results may differ from the reference program's by a relative error of at most 0.015.
Values may be sent and summed in bfloat16 or wider, within the bound.
No kernel may reach another device: no remote copies, remote signals or barrier semaphores. Data moves between devices by JAX's collectives and lax.ppermute only.
A program may use at most 64 MiB of HBM per device.

```python
import jax
import jax.numpy as jnp
from jax import lax

D = 512
HEADS = 4
MAXLEN = 256
NSEQ = 8
ROWS_DEV = 1024
SLOTS = 4
UNIQ = 256
ROWS = 131072
SLOTS_ALL = 1024
N_SEQ = 4
DEVICES = 128


def draw_unique_ids(key, part):
    stripe = ROWS_DEV // SLOTS

    def per_device(dev_key):
        key_off, key_pick, key_full, key_order = jax.random.split(dev_key, 4)
        offsets = jax.random.randint(key_off, (DEVICES, SLOTS), 0, stripe)
        local_rows = jnp.arange(SLOTS, dtype=jnp.int32)[None, :] * stripe + offsets
        id_grid = jnp.arange(DEVICES, dtype=jnp.int32)[:, None] * ROWS_DEV + local_rows
        scores = jax.random.randint(key_pick, (DEVICES, SLOTS), 0, 1 << 16) * (DEVICES * SLOTS)
        scores = scores + jnp.arange(DEVICES * SLOTS, dtype=jnp.int32).reshape(DEVICES, SLOTS)
        full_owner = jax.random.randint(key_full, (), 0, DEVICES)
        boosted = jnp.arange(DEVICES, dtype=jnp.int32)[:, None] == full_owner
        scores = jnp.where(boosted, scores + (1 << 16) * (DEVICES * SLOTS), scores)
        picked = lax.top_k(scores.reshape(-1), UNIQ)[1]
        chosen_ids = id_grid.reshape(-1)[picked]
        return chosen_ids[jax.random.permutation(key_order, UNIQ)]
    device_keys = jax.vmap(lambda device: jax.random.fold_in(key, device))(jnp.arange(DEVICES))
    return jax.vmap(per_device)(device_keys).reshape(-1).astype(jnp.int32)


def draw_inverse(key, part):
    early = MAXLEN // 4

    def per_device(dev_key):
        random_key_root, key_perm = jax.random.split(dev_key)
        base = jax.random.randint(random_key_root, (NSEQ, MAXLEN), 0, UNIQ)
        order = jax.random.permutation(key_perm, UNIQ)
        flat = jnp.arange(NSEQ, dtype=jnp.int32)[:, None] * early + jnp.arange(MAXLEN, dtype=jnp.int32)[None, :]
        forced = (jnp.arange(MAXLEN, dtype=jnp.int32)[None, :] < early) & (flat < UNIQ)
        return jnp.where(forced, order[jnp.minimum(flat, UNIQ - 1)], base)
    device_keys = jax.vmap(lambda device: jax.random.fold_in(key, device))(jnp.arange(DEVICES))
    return jax.vmap(per_device)(device_keys).reshape(DEVICES * NSEQ, MAXLEN).astype(jnp.int32)


def slot_plan(key):
    plan_key = jax.random.fold_in(key, 7)
    groups = DEVICES // N_SEQ
    key_heavy, key_long, key_short, key_top = jax.random.split(plan_key, 4)
    heavy = jax.random.randint(key_heavy, (groups,), 0, N_SEQ)
    long_len = jax.random.randint(key_long, (groups, N_SEQ, NSEQ), MAXLEN // 2, MAXLEN + 1)
    short_len = jax.random.randint(key_short, (groups, N_SEQ, NSEQ), MAXLEN // 4, MAXLEN // 2 + 1)
    is_heavy = jnp.arange(N_SEQ, dtype=jnp.int32)[None, :, None] == heavy[:, None, None]
    slot_lens = jnp.where(is_heavy, long_len, short_len)
    top_slot = jax.random.randint(key_top, (groups,), 0, NSEQ)
    is_top = is_heavy & (jnp.arange(NSEQ, dtype=jnp.int32)[None, None, :] == top_slot[:, None, None])
    slot_lens = jnp.where(is_top, MAXLEN, slot_lens)
    order_key = (MAXLEN - slot_lens) * NSEQ + jnp.arange(NSEQ, dtype=jnp.int32)[None, None, :]
    order = jnp.argsort(order_key, axis=-1)
    slot_rank = jnp.argsort(order, axis=-1).astype(jnp.int32)
    source = jnp.arange(N_SEQ, dtype=jnp.int32)[None, :, None]
    target = (source + slot_rank) % N_SEQ
    per_partner = NSEQ // N_SEQ
    placed = target * NSEQ + source * per_partner + slot_rank // N_SEQ
    return (slot_lens.reshape(-1).astype(jnp.int32), placed.reshape(-1).astype(jnp.int32))


def draw_lengths(key, part):
    return slot_plan(key)[0]


def draw_assignment(key, part):
    return slot_plan(key)[1]


def shard_levels(own_key, extent, shards, least, high):
    level = 1.0
    for axis_at, shards_of in shards:
        heights = jax.random.uniform(jax.random.fold_in(jax.random.fold_in(own_key, 6), axis_at), (shards_of,), jnp.float32, least / len(shards), high / len(shards))
        level = level * jnp.repeat(jnp.exp(heights), extent[axis_at] // shards_of).reshape((-1,) + (1,) * (len(extent) - 1 - axis_at))
    return level


def scatter_about(own_key, extent, width, reach, shards=(), held_as=jnp.bfloat16):
    values = width * jax.random.normal(own_key, extent, jnp.float32)
    if shards:
        values = values * shard_levels(own_key, extent, shards, -0.22, 0.18)
    return jnp.clip(values, -reach, reach).astype(held_as)


def setup_inputs(seed: int = 0) -> dict:
    keys = jax.random.split(jax.random.key(seed), 13)
    return {
        "item_table": scatter_about(keys[0], (ROWS, D), 1.0, 6.0, ((0, 128),)),
        "unique_ids": draw_unique_ids(jax.random.fold_in(keys[12], 71), 0),
        "inverse": draw_inverse(jax.random.fold_in(keys[12], 71), 0),
        "lengths": draw_lengths(jax.random.fold_in(keys[12], 71), 0),
        "assignment": draw_assignment(jax.random.fold_in(keys[12], 71), 0),
        "proj_in": scatter_about(keys[5], (D, 4 * D), D ** -0.5, 0.25),
        "bias_in": scatter_about(keys[6], (4 * D,), 0.5, 3.0, (), jnp.float32),
        "gain_in": jnp.clip(1.0 + 0.18 * jax.random.normal(keys[7], (D,), jnp.float32), 0.1, 1.9),
        "gain_mid": jnp.clip(1.0 + 0.18 * jax.random.normal(keys[8], (D,), jnp.float32), 0.1, 1.9),
        "proj_out": scatter_about(keys[9], (D, D), D ** -0.5, 0.25),
        "position_bias": scatter_about(keys[10], (HEADS, MAXLEN), 1.0, 4.0, (), jnp.float32),
        "cotangent": scatter_about(keys[11], (SLOTS_ALL, MAXLEN, D), 1.0, 6.0, ((0, 128),)),
    }


def layer_norm(values, gain):
    center = values - lax.optimization_barrier(jnp.mean(values, axis=-1, keepdims=True))
    spread = lax.optimization_barrier(jnp.mean(center * center, axis=-1, keepdims=True))
    return center * lax.rsqrt(spread + 1e-05) * gain

def relative_table(position_bias, length):
    row_pos = jnp.arange(length, dtype=jnp.int32)
    distance = jnp.clip(row_pos[:, None] - row_pos[None, :], 0, length - 1)
    return position_bias[:, distance]

def slot_layer(inputs, seq_len, proj_in, bias_in, gain_in, gain_mid, proj_out, toeplitz):
    length = inputs.shape[0]
    feature = inputs.shape[1]
    head_count = toeplitz.shape[0]
    head_size = feature // head_count
    normed = layer_norm(inputs.astype(jnp.float32), gain_in).astype(jnp.bfloat16)
    hidden = jax.nn.silu(jnp.dot(normed, proj_in, preferred_element_type=jnp.float32) + bias_in).astype(jnp.bfloat16)
    gate_portion = hidden[:, :feature]
    value_part = hidden[:, feature:2 * feature].reshape(length, head_count, head_size).astype(jnp.float32)
    query_part = hidden[:, 2 * feature:3 * feature].reshape(length, head_count, head_size).astype(jnp.float32)
    key_part = hidden[:, 3 * feature:].reshape(length, head_count, head_size).astype(jnp.float32)
    scores = jnp.einsum('ihe,jhe->hij', query_part, key_part) * head_size ** (-0.5) + toeplitz
    row_pos = jnp.arange(length, dtype=jnp.int32)[:, None]
    col_pos = jnp.arange(length, dtype=jnp.int32)[None, :]
    allowed = (col_pos <= row_pos) & (row_pos < seq_len)
    weights = jnp.where(allowed[None], jax.nn.silu(scores) / seq_len.astype(jnp.float32), 0.0).astype(jnp.bfloat16)
    mixed_heads = jnp.einsum('hij,jhe->ihe', weights.astype(jnp.float32), value_part).reshape(length, feature)
    gated_out = (layer_norm(mixed_heads, gain_mid) * gate_portion.astype(jnp.float32)).astype(jnp.bfloat16)
    result = inputs.astype(jnp.float32) + jnp.dot(gated_out, proj_out, preferred_element_type=jnp.float32)
    return jnp.where(row_pos < seq_len, result, 0.0).astype(jnp.bfloat16)

def slot_step(slot_in, seq_len, grad_out, proj_in, bias_in, gain_in, gain_mid, proj_out, toeplitz):
    result, pullback = jax.vjp(lambda inputs: slot_layer(inputs, seq_len, proj_in, bias_in, gain_in, gain_mid, proj_out, toeplitz), slot_in)
    return (result, pullback(grad_out)[0])

def reference(item_table, unique_ids, inverse, lengths, assignment, proj_in, bias_in, gain_in, gain_mid, proj_out, position_bias, cotangent):
    fetched = item_table[unique_ids]
    slot_total = DEVICES * NSEQ
    device_of = jnp.arange(slot_total, dtype=jnp.int32) // NSEQ
    token_ids = inverse + (device_of * UNIQ)[:, None]
    position = jnp.arange(MAXLEN, dtype=jnp.int32)
    in_range = position[None, :] < lengths[:, None]
    home_rows = jnp.where(in_range[:, :, None], fetched[token_ids], jnp.zeros((), jnp.bfloat16))
    destination = device_of // N_SEQ * (N_SEQ * NSEQ) + assignment
    balanced = jnp.zeros_like(home_rows).at[destination].set(home_rows)
    count_totals = jnp.zeros((slot_total,), jnp.int32).at[destination].set(lengths)
    toeplitz = relative_table(position_bias, MAXLEN)
    outputs, token_grads = lax.map(lambda packed: slot_step(packed[0], packed[1], packed[2], proj_in, bias_in, gain_in, gain_mid, proj_out, toeplitz), (balanced, count_totals, cotangent))
    home_grads = token_grads[destination].astype(jnp.float32)
    row_gradient_list = jnp.zeros((DEVICES * UNIQ, D), jnp.float32).at[token_ids].add(home_grads)
    table_grad = jnp.zeros((ROWS_DEV * DEVICES, D), jnp.float32).at[unique_ids].add(row_gradient_list)
    return (outputs, table_grad)
```

```python
import functools

import jax
import jax.numpy as jnp
from jax import lax
from jax.experimental import pallas as pl
from jax.experimental.pallas import tpu as pltpu
from jax.sharding import PartitionSpec as P

D = 512
HEADS = 4
HEAD = 128
MAXLEN = 256
UNIQ = 256
ROWS_DEV = 1024
DEVICES = 128
SCALE = HEAD**-0.5
EPS = 1e-05
MASKED = -1e30
BF = jnp.bfloat16
F32 = jnp.float32
I32 = jnp.int32


def nn(a, b):
    return lax.dot_general(a, b, (((1,), (0,)), ((), ())), preferred_element_type=F32)


def nt(a, b):
    return lax.dot_general(a, b, (((1,), (1,)), ((), ())), preferred_element_type=F32)


def tn(a, b):
    return lax.dot_general(a, b, (((0,), (0,)), ((), ())), preferred_element_type=F32)


def iota(shape, dim):
    return lax.broadcasted_iota(I32, shape, dim)


def onehot(mask):
    return jnp.where(mask, 1.0, 0.0).astype(BF)


def params(**kw):
    return pltpu.CompilerParams(vmem_limit_bytes=48 << 20, **kw)


def pack_kernel(assign_ref, len_ref, seq_ref, ids_ref, inv_ref, req_ref, pos_ref, *msg_refs):
    ids = ids_ref[...]
    owner = ids >> 10
    local = (ids & (ROWS_DEV - 1)).astype(F32)
    held = iota((DEVICES, UNIQ), 0) == owner
    earlier = onehot(iota((UNIQ, UNIQ), 0) < iota((UNIQ, UNIQ), 1))
    before = nn(onehot(held), earlier)
    rank = jnp.sum(jnp.where(held, before, 0.0), axis=0, keepdims=True)
    pos_ref[...] = owner * 8 + rank.astype(I32)
    lane = iota((DEVICES, 4), 1)
    req = jnp.zeros((DEVICES, 4), F32)
    for r in range(4):
        chosen = held & (before == float(r))
        col = jnp.sum(jnp.where(chosen, ROWS_DEV - local, 0.0), axis=1, keepdims=True)
        req = jnp.where(lane == r, ROWS_DEV - col, req)
    req_ref[...] = req.astype(I32)
    seq = seq_ref[0]
    for j in range(8):
        place = assign_ref[j]
        delta = (place // 8 - seq + 4) % 4
        half = place % 2
        row = jnp.concatenate(
            [inv_ref[j : j + 1, :], jnp.full((1, 128), len_ref[j], I32)], axis=1
        )
        for d in range(4):
            for b in range(2):

                @pl.when((delta == d) & (half == b))
                def _():
                    msg_refs[d][b : b + 1, :] = row


def pack(assignment, lengths, seq, ids, inverse):
    smem = pl.BlockSpec(memory_space=pltpu.SMEM)
    vmem = pl.BlockSpec(memory_space=pltpu.VMEM)
    return pl.pallas_call(
        pack_kernel,
        in_specs=[smem, smem, smem, vmem, vmem],
        out_specs=[vmem] * 6,
        out_shape=[
            jax.ShapeDtypeStruct((DEVICES, 4), I32),
            jax.ShapeDtypeStruct((1, UNIQ), I32),
        ]
        + [jax.ShapeDtypeStruct((2, MAXLEN + 128), I32)] * 4,
        compiler_params=params(),
        name="pack",
    )(assignment, lengths, seq, ids.reshape(1, UNIQ), inverse)


def tables_kernel(flipped_ref, pos_ref, bias_ref, pos_rows_ref):
    i = iota((MAXLEN, MAXLEN), 0)
    j = iota((MAXLEN, MAXLEN), 1)
    for h in range(HEADS):
        line = jnp.broadcast_to(flipped_ref[h : h + 1, :], (MAXLEN, MAXLEN))
        spread = pltpu.roll(line, 1, 1, stride=1, stride_axis=0)
        full = jnp.where(j <= i, 0.5 * spread, MASKED)
        bias_ref[h] = full[:, :128]
    pos = jnp.broadcast_to(pos_ref[...], (UNIQ, UNIQ)).astype(F32)
    col = jnp.sum(jnp.where(i == j, pos, 0.0), axis=1, keepdims=True)
    pos_rows_ref[...] = jnp.broadcast_to(col.astype(I32), (UNIQ, 128))


def tables(position_bias, pos):
    return pl.pallas_call(
        tables_kernel,
        out_shape=[
            jax.ShapeDtypeStruct((HEADS, MAXLEN, 128), F32),
            jax.ShapeDtypeStruct((UNIQ, 128), I32),
        ],
        compiler_params=params(),
        name="tables",
    )(position_bias[:, ::-1], pos)


def asked_parts(asked_ref):
    asked = asked_ref[...]
    return (asked >> 5).astype(BF), (asked & 31).astype(BF)


def answer_kernel(asked_ref, table_ref, out_ref):
    high, low = asked_parts(asked_ref)
    count = 256
    for c in range(8 * DEVICES // count):
        row = iota((count, DEVICES), 0) + c * count
        spread = onehot((row >> 3) == iota((count, DEVICES), 1))
        value = nn(spread, high) * 32.0 + nn(spread, low)
        rank = (iota((count, 4), 0)) & 3
        col = jnp.sum(jnp.where(iota((count, 4), 1) == rank, value, 0.0), axis=1, keepdims=True)
        pick = onehot(iota((count, ROWS_DEV), 1) == col.astype(I32))
        both = nn(pick, table_ref[...])
        upper = (iota((count, D // 2), 0) & 7) < 4
        out_ref[pl.ds(c * count, count), :] = jnp.where(
            upper, both[:, : D // 2], both[:, D // 2 :]
        ).astype(BF)


def answer_rows(asked, table):
    return pl.pallas_call(
        answer_kernel,
        out_shape=jax.ShapeDtypeStruct((8 * DEVICES, D // 2), BF),
        compiler_params=params(),
        name="answer",
    )(asked, table)


def compact_kernel(pos_ref, got_ref, out_ref):
    pos = pos_ref[:, :1]
    lane = iota((UNIQ, 8 * DEVICES), 1)
    for half in range(2):
        pick = onehot(lane == pos + 4 * half)
        out_ref[:, pl.ds(half * 256, 256)] = nn(pick, got_ref[...]).astype(BF)


def compact(pos_rows, got):
    return pl.pallas_call(
        compact_kernel,
        out_shape=jax.ShapeDtypeStruct((UNIQ, D), BF),
        compiler_params=params(),
        name="compact",
    )(pos_rows, got)


def row_mean(x):
    return jnp.sum(x, axis=-1, keepdims=True) * (1.0 / D)


def norm_parts(x):
    center = x - row_mean(x)
    spread = row_mean(center * center)
    inv = lax.rsqrt(spread + EPS)
    return center * inv, inv


def norm_grad(g, unit, inv):
    return inv * (g - row_mean(g) - unit * row_mean(g * unit))


def slot_body(size, count, ids, rows, cot, out_ref, acc_ref, fresh, refs):
    (win_ref, bin_ref, gin_ref, gmid_ref, wout_ref, bias_ref, hid, slope, wts, wslope, dpre, mix) = refs
    rowpos = iota((size, 1), 0)
    valid = rowpos < count
    ids_rows = jnp.broadcast_to(ids[:, :size], (8, size)).astype(F32)
    ids_cols = ids_rows.T[:, :1].astype(I32)
    pick = onehot((iota((size, UNIQ), 1) == ids_cols) & valid)
    x = nn(pick, rows)
    unit_in, inv_in = norm_parts(x)
    normed = (unit_in * gin_ref[...]).astype(BF)
    for c in range(4):
        cols = pl.ds(c * D, D)
        half = 0.5 * (nn(normed, win_ref[:, cols]) + bin_ref[:, cols])
        up = 1.0 + jnp.tanh(half)
        act = half * up
        hid[:size, cols] = act.astype(BF)
        slope[:size, cols] = 0.5 * (up + act * (2.0 - up))
    per = jnp.where(valid, 1.0, 0.0) / count.astype(F32)
    blocks = size // 128
    for h in range(HEADS):
        vcol, qcol, kcol = (pl.ds(D * g + h * HEAD, HEAD) for g in (1, 2, 3))
        for bi in range(blocks):
            rs = pl.ds(bi * 128, 128)
            width = (bi + 1) * 128
            if bi == 0:
                bias = bias_ref[h, :128, :]
            else:
                bias = jnp.concatenate([bias_ref[h, 128:, :], bias_ref[h, :128, :]], axis=1)
            half = nt(hid[rs, qcol], hid[:width, kcol]) * (0.5 * SCALE) + bias
            up = 1.0 + jnp.tanh(half)
            act = half * up
            scale = per[bi * 128 : (bi + 1) * 128]
            w = (act * scale).astype(BF)
            wts[h, rs, :width] = w
            wslope[h, rs, :width] = (up + act * (2.0 - up)) * (scale * (0.5 * SCALE))
            mix[rs, pl.ds(h * HEAD, HEAD)] = nn(w, hid[:width, vcol])
    unit_mid, inv_mid = norm_parts(mix[:size, :])
    scaled = unit_mid * gmid_ref[...]
    gate = hid[:size, :D].astype(F32)
    gated = (scaled * gate).astype(BF)
    result = x + nn(gated, wout_ref[...])
    out_ref[0, :size, :] = jnp.where(valid, result, 0.0).astype(BF)
    if size < MAXLEN:
        out_ref[0, size:, :] = jnp.zeros((MAXLEN - size, D), BF)
    grad = jnp.where(valid, cot.astype(F32), 0.0)
    dgated = nt(grad.astype(BF), wout_ref[...]).astype(BF).astype(F32)
    dgate = (dgated * scaled).astype(BF).astype(F32)
    dpre[:size, :D] = (dgate * slope[:size, :D]).astype(BF)
    dmix = norm_grad(dgated * gate * gmid_ref[...], unit_mid, inv_mid).astype(BF)
    for h in range(HEADS):
        vcol, qcol, kcol = (pl.ds(D * g + h * HEAD, HEAD) for g in (1, 2, 3))
        dv = [None] * blocks
        dk = [None] * blocks
        for bi in range(blocks):
            rs = pl.ds(bi * 128, 128)
            width = (bi + 1) * 128
            dm = dmix[bi * 128 : (bi + 1) * 128, h * HEAD : (h + 1) * HEAD]
            dw = nt(dm, hid[:width, vcol])
            ds = (dw * wslope[h, rs, :width]).astype(BF)
            dq = nn(ds, hid[:width, kcol]).astype(BF).astype(F32)
            dpre[rs, qcol] = (dq * slope[rs, qcol]).astype(BF)
            dvs = tn(wts[h, rs, :width], dm)
            dks = tn(ds, hid[rs, qcol])
            for bj in range(bi + 1):
                part = slice(bj * 128, (bj + 1) * 128)
                dv[bj] = dvs[part] if dv[bj] is None else dv[bj] + dvs[part]
                dk[bj] = dks[part] if dk[bj] is None else dk[bj] + dks[part]
        for bj in range(blocks):
            rs = pl.ds(bj * 128, 128)
            dpre[rs, vcol] = (dv[bj].astype(BF).astype(F32) * slope[rs, vcol]).astype(BF)
            dpre[rs, kcol] = (dk[bj].astype(BF).astype(F32) * slope[rs, kcol]).astype(BF)
    dnormed = nt(dpre[:size, :], win_ref[...]).astype(BF).astype(F32)
    dx = norm_grad(dnormed * gin_ref[...], unit_in, inv_in)
    token = (dx + grad).astype(BF)
    back = onehot((iota((UNIQ, size), 0) == ids[:, :size]) & (iota((UNIQ, size), 1) < count))
    sums = nn(back, token)
    acc_ref[...] = jnp.where(fresh, sums, sums + acc_ref[...])


def layer_kernel(plan, aliased, *refs):
    deltas, each = plan
    n_src = len(deltas)
    refs = list(refs)
    seq_ref = refs.pop(0)
    smsg = [refs.pop(0) for _ in range(n_src)]
    vmsg = [refs.pop(0) for _ in range(n_src)]
    rows_refs = [refs.pop(0) for _ in range(n_src)]
    cot_ref = refs.pop(0)
    win_ref, bin_ref, gin_ref, gmid_ref, wout_ref, bias_ref = (refs.pop(0) for _ in range(6))
    if aliased:
        refs.pop(0)
    out_ref = refs.pop(0)
    part_refs = [refs.pop(0) for _ in range(n_src)]
    rows, ids_sc, acc = (refs.pop(0) for _ in range(3))
    scratch = refs
    step = pl.program_id(0)
    src = step // len(each)
    turn = step % len(each)
    count = jnp.int32(0)
    for d in range(n_src):
        for t, b in enumerate(each):
            here = (src == d) & (turn == t)
            count = jnp.where(here, smsg[d][b, MAXLEN], count)

            @pl.when(here)
            def _():
                ids_sc[...] = vmsg[d][b : b + 1, :MAXLEN]
                if t == 0:
                    rows[...] = rows_refs[d][...]

    weights = (win_ref, bin_ref, gin_ref, gmid_ref, wout_ref, bias_ref, *scratch)
    for size in (128, 256):

        @pl.when((count <= 128) == (size == 128))
        def _():
            slot_body(
                size,
                count,
                ids_sc[...],
                rows[...],
                cot_ref[0, :size, :],
                out_ref,
                acc,
                turn == 0,
                weights,
            )

    for d in range(n_src):

        @pl.when((src == d) & (turn == len(each) - 1))
        def _():
            part_refs[d][...] = acc[...].astype(BF)


def layer(plan, seq, msgs, rows, cot, weights, prior):
    deltas, each = plan
    n_src = len(deltas)
    n_each = len(each)

    def slot(i, seq_ref):
        src = i // n_each
        delta = deltas[0]
        for d in range(1, n_src):
            delta = jnp.where(src == d, deltas[d], delta)
        turn = i % n_each
        b = each[0]
        for t in range(1, n_each):
            b = jnp.where(turn == t, each[t], b)
        return ((seq_ref[0] - delta + 4) % 4) * 2 + b, 0, 0

    whole = lambda a: pl.BlockSpec(a.shape, lambda i, s, n=a.ndim: (0,) * n, pipeline_mode=pl.Buffered(1))
    smem = pl.BlockSpec(memory_space=pltpu.SMEM)
    in_specs = [smem] * n_src + [whole(m) for m in msgs] + [whole(r) for r in rows]
    in_specs += [pl.BlockSpec((1, MAXLEN, D), slot)] + [whole(w) for w in weights]
    args = [*msgs, *msgs, *rows, cot, *weights]
    alias = {}
    if prior is not None:
        in_specs.append(pl.BlockSpec(memory_space=pl.ANY))
        args.append(prior)
        alias = {len(args): 0}
    part = jax.ShapeDtypeStruct((UNIQ, D), BF)
    return pl.pallas_call(
        functools.partial(layer_kernel, plan, prior is not None),
        grid_spec=pltpu.PrefetchScalarGridSpec(
            num_scalar_prefetch=1,
            grid=(n_src * n_each,),
            in_specs=in_specs,
            out_specs=[pl.BlockSpec((1, MAXLEN, D), slot)]
            + [pl.BlockSpec((UNIQ, D), lambda i, s: (0, 0))] * n_src,
            scratch_shapes=[
                pltpu.VMEM((UNIQ, D), BF),
                pltpu.VMEM((1, MAXLEN), I32),
                pltpu.VMEM((UNIQ, D), F32),
                pltpu.VMEM((MAXLEN, 4 * D), BF),
                pltpu.VMEM((MAXLEN, 4 * D), F32),
                pltpu.VMEM((HEADS, MAXLEN, MAXLEN), BF),
                pltpu.VMEM((HEADS, MAXLEN, MAXLEN), F32),
                pltpu.VMEM((MAXLEN, 4 * D), BF),
                pltpu.VMEM((MAXLEN, D), F32),
            ],
        ),
        out_shape=[jax.ShapeDtypeStruct(cot.shape, BF)] + [part] * n_src,
        input_output_aliases=alias,
        compiler_params=params(dimension_semantics=("arbitrary",)),
        name="layer",
    )(seq, *args)


def expand_kernel(pos_ref, *refs):
    out_ref = refs[-1]
    total = refs[0][...].astype(F32)
    for r in refs[1:-1]:
        total = total + r[...].astype(F32)
    total = total.astype(BF)
    row = iota((8 * DEVICES, UNIQ), 0)
    pos = pos_ref[...]
    upper = nn(onehot(row == pos), total[:, : D // 2])
    lower = nn(onehot(row == pos + 4), total[:, D // 2 :])
    out_ref[...] = (upper + lower).astype(BF)


def expand(pos, parts):
    return pl.pallas_call(
        expand_kernel,
        out_shape=jax.ShapeDtypeStruct((8 * DEVICES, D // 2), BF),
        compiler_params=params(),
        name="expand",
    )(pos, *parts)


def asked_line_kernel(asked_ref, out_ref):
    parts = []
    spread = onehot(iota((DEVICES, 8 * DEVICES), 0) == (iota((DEVICES, 8 * DEVICES), 1) >> 3))
    for part in asked_parts(asked_ref):
        square = jnp.concatenate([part.astype(F32), jnp.zeros((DEVICES, 124), F32)], axis=1)
        parts.append(nn(square.T[:8].astype(BF), spread))
    value = parts[0] * 32.0 + parts[1]
    mine = iota((8, 8 * DEVICES), 0) == (iota((8, 8 * DEVICES), 1) & 3)
    out_ref[...] = jnp.sum(jnp.where(mine, value, 0.0), axis=0, keepdims=True).astype(I32)


def asked_line(asked):
    return pl.pallas_call(
        asked_line_kernel,
        out_shape=jax.ShapeDtypeStruct((1, 8 * DEVICES), I32),
        compiler_params=params(),
        name="asked_line",
    )(asked)


def scatter_kernel(line_ref, landed_ref, out_ref):
    size = out_ref.shape[0]
    row = iota((size, 8 * DEVICES), 0) + pl.program_id(0) * size
    upper = (iota((1, 8 * DEVICES), 1) & 7) < 4
    line = line_ref[...]
    for half in range(2):
        wanted = jnp.where(upper == (half == 0), line, -1)
        out_ref[:, pl.ds(half * 256, 256)] = nn(onehot(row == wanted), landed_ref[...])


def scatter(line, landed):
    size = 256
    whole = lambda a: pl.BlockSpec(a.shape, lambda i: (0, 0), pipeline_mode=pl.Buffered(1))
    return pl.pallas_call(
        scatter_kernel,
        grid=(ROWS_DEV // size,),
        in_specs=[whole(line), whole(landed)],
        out_specs=pl.BlockSpec((size, D), lambda i: (i, 0)),
        out_shape=jax.ShapeDtypeStruct((ROWS_DEV, D), F32),
        compiler_params=params(dimension_semantics=("arbitrary",)),
        name="scatter",
    )(line, landed)


def ring(delta):
    return [(i, (i + delta) % 4) for i in range(4)]


def exchange(x, shape):
    got = lax.all_to_all(x.reshape(shape), ("emb", "seq"), split_axis=0, concat_axis=0, tiled=True)
    return got.reshape(x.shape)


PLANS = (((0, 1, 3, 2), (0, 1)),)


def shards(
    item_table,
    unique_ids,
    inverse,
    lengths,
    assignment,
    proj_in,
    bias_in,
    gain_in,
    gain_mid,
    proj_out,
    position_bias,
    cotangent,
):
    seq = lax.axis_index("seq").astype(I32).reshape(1)
    req, pos, *sent = pack(assignment, lengths, seq, unique_ids, inverse)
    asked = exchange(req, (DEVICES, 1, 4))
    msgs = [sent[0]] + [lax.ppermute(sent[d], "seq", ring(d)) for d in (1, 2, 3)]
    bias, pos_rows = tables(position_bias, pos)
    answer = answer_rows(asked, item_table)
    got = exchange(answer, (DEVICES, 8, D // 2))
    line = asked_line(asked)
    own = compact(pos_rows, got)
    rows = [own] + [lax.ppermute(own, "seq", ring(d)) for d in (1, 2, 3)]
    weights = (
        proj_in,
        bias_in.reshape(1, 4 * D),
        gain_in.reshape(1, D),
        gain_mid.reshape(1, D),
        proj_out,
        bias,
    )
    outputs = None
    sums = []
    for plan in PLANS:
        outputs, *parts = layer(
            plan,
            seq,
            [msgs[d] for d in plan[0]],
            [rows[d] for d in plan[0]],
            cotangent,
            weights,
            outputs,
        )
        for d, part in zip(plan[0], parts):
            sums.append(part if d == 0 else lax.ppermute(part, "seq", ring(-d)))
    landed = exchange(expand(pos, sums), (DEVICES, 8, D // 2))
    return (outputs, scatter(line, landed))


def solution(mesh):
    both = ("emb", "seq")
    in_specs = (
        P(both, None),
        P(both),
        P(both, None),
        P(both),
        P(both),
        P(),
        P(),
        P(),
        P(),
        P(),
        P(),
        P(both, None, None),
    )
    out_specs = (P(both, None, None), P(both, None))
    return jax.shard_map(shards, mesh=mesh, in_specs=in_specs, out_specs=out_specs, check_vma=False)
```

```python
import functools

import jax
import jax.numpy as jnp
from jax import lax
from jax.experimental import pallas as pl
from jax.experimental.pallas import tpu as pltpu
from jax.sharding import PartitionSpec as P

D = 512
HEADS = 4
HEAD = 128
MAXLEN = 256
UNIQ = 256
ROWS_DEV = 1024
DEVICES = 128
SCALE = HEAD**-0.5
EPS = 1e-05
MASKED = -1e30
BF = jnp.bfloat16
F32 = jnp.float32
I32 = jnp.int32


def nn(a, b):
    return lax.dot_general(a, b, (((1,), (0,)), ((), ())), preferred_element_type=F32)


def nt(a, b):
    return lax.dot_general(a, b, (((1,), (1,)), ((), ())), preferred_element_type=F32)


def tn(a, b):
    return lax.dot_general(a, b, (((0,), (0,)), ((), ())), preferred_element_type=F32)


def iota(shape, dim):
    return lax.broadcasted_iota(I32, shape, dim)


def onehot(mask):
    return jnp.where(mask, 1.0, 0.0).astype(BF)


def params(**kw):
    return pltpu.CompilerParams(vmem_limit_bytes=24 << 20, **kw)


def pack_kernel(assign_ref, len_ref, seq_ref, ids_ref, inv_ref, req_ref, pos_ref, *msg_refs):
    ids = ids_ref[...]
    owner = ids >> 10
    local = (ids & (ROWS_DEV - 1)).astype(F32)
    held = iota((DEVICES, UNIQ), 0) == owner
    earlier = onehot(iota((UNIQ, UNIQ), 0) < iota((UNIQ, UNIQ), 1))
    before = nn(onehot(held), earlier)
    rank = jnp.sum(jnp.where(held, before, 0.0), axis=0, keepdims=True)
    pos_ref[...] = owner * 8 + rank.astype(I32)
    lane = iota((DEVICES, 4), 1)
    req = jnp.zeros((DEVICES, 4), F32)
    for r in range(4):
        chosen = held & (before == float(r))
        col = jnp.sum(jnp.where(chosen, ROWS_DEV - local, 0.0), axis=1, keepdims=True)
        req = jnp.where(lane == r, ROWS_DEV - col, req)
    req_ref[...] = req.astype(I32)
    seq = seq_ref[0]
    for j in range(8):
        place = assign_ref[j]
        delta = (place // 8 - seq + 4) % 4
        half = place % 2
        row = jnp.concatenate(
            [inv_ref[j : j + 1, :], jnp.full((1, 128), len_ref[j], I32)], axis=1
        )
        for d in range(4):
            for b in range(2):

                @pl.when((delta == d) & (half == b))
                def _():
                    msg_refs[d][b : b + 1, :] = row


def pack(assignment, lengths, seq, ids, inverse):
    smem = pl.BlockSpec(memory_space=pltpu.SMEM)
    vmem = pl.BlockSpec(memory_space=pltpu.VMEM)
    return pl.pallas_call(
        pack_kernel,
        in_specs=[smem, smem, smem, vmem, vmem],
        out_specs=[vmem] * 6,
        out_shape=[
            jax.ShapeDtypeStruct((DEVICES, 4), I32),
            jax.ShapeDtypeStruct((1, UNIQ), I32),
        ]
        + [jax.ShapeDtypeStruct((2, MAXLEN + 128), I32)] * 4,
        compiler_params=params(),
        name="pack",
    )(assignment, lengths, seq, ids.reshape(1, UNIQ), inverse)


def tables_kernel(flipped_ref, pos_ref, bias_ref, pos_rows_ref):
    i = iota((MAXLEN, MAXLEN), 0)
    j = iota((MAXLEN, MAXLEN), 1)
    for h in range(HEADS):
        line = jnp.broadcast_to(flipped_ref[h : h + 1, :], (MAXLEN, MAXLEN))
        spread = pltpu.roll(line, 1, 1, stride=1, stride_axis=0)
        full = jnp.where(j <= i, 0.5 * spread, MASKED)
        bias_ref[h] = full[:, :128]
    pos = jnp.broadcast_to(pos_ref[...], (UNIQ, UNIQ)).astype(F32)
    col = jnp.sum(jnp.where(i == j, pos, 0.0), axis=1, keepdims=True)
    pos_rows_ref[...] = jnp.broadcast_to(col.astype(I32), (UNIQ, 128))


def tables(position_bias, pos):
    return pl.pallas_call(
        tables_kernel,
        out_shape=[
            jax.ShapeDtypeStruct((HEADS, MAXLEN, 128), F32),
            jax.ShapeDtypeStruct((UNIQ, 128), I32),
        ],
        compiler_params=params(),
        name="tables",
    )(position_bias[:, ::-1], pos)


def asked_parts(asked_ref):
    asked = asked_ref[...]
    return (asked >> 5).astype(BF), (asked & 31).astype(BF)


def answer_kernel(asked_ref, table_ref, out_ref):
    high, low = asked_parts(asked_ref)
    count = 256
    for c in range(8 * DEVICES // count):
        row = iota((count, DEVICES), 0) + c * count
        spread = onehot((row >> 3) == iota((count, DEVICES), 1))
        value = nn(spread, high) * 32.0 + nn(spread, low)
        rank = (iota((count, 4), 0)) & 3
        col = jnp.sum(jnp.where(iota((count, 4), 1) == rank, value, 0.0), axis=1, keepdims=True)
        pick = onehot(iota((count, ROWS_DEV), 1) == col.astype(I32))
        both = nn(pick, table_ref[...])
        upper = (iota((count, D // 2), 0) & 7) < 4
        out_ref[pl.ds(c * count, count), :] = jnp.where(
            upper, both[:, : D // 2], both[:, D // 2 :]
        ).astype(BF)


def answer_rows(asked, table):
    return pl.pallas_call(
        answer_kernel,
        out_shape=jax.ShapeDtypeStruct((8 * DEVICES, D // 2), BF),
        compiler_params=params(),
        name="answer",
    )(asked, table)


def compact_kernel(pos_ref, got_ref, out_ref):
    pos = pos_ref[:, :1]
    lane = iota((UNIQ, 8 * DEVICES), 1)
    for half in range(2):
        pick = onehot(lane == pos + 4 * half)
        out_ref[:, pl.ds(half * 256, 256)] = nn(pick, got_ref[...]).astype(BF)


def compact(pos_rows, got):
    return pl.pallas_call(
        compact_kernel,
        out_shape=jax.ShapeDtypeStruct((UNIQ, D), BF),
        compiler_params=params(),
        name="compact",
    )(pos_rows, got)


def row_mean(x):
    return jnp.sum(x, axis=-1, keepdims=True) * (1.0 / D)


def norm_parts(x):
    center = x - row_mean(x)
    spread = row_mean(center * center)
    inv = lax.rsqrt(spread + EPS)
    return center * inv, inv


def norm_grad(g, unit, inv):
    return inv * (g - row_mean(g) - unit * row_mean(g * unit))


def slot_body(size, count, ids, rows, cot, out_ref, acc_ref, fresh, refs):
    (win_ref, bin_ref, gin_ref, gmid_ref, wout_ref, bias_ref, hid, slope, wts, wslope, dpre, mix) = refs
    rowpos = iota((size, 1), 0)
    valid = rowpos < count
    ids_rows = jnp.broadcast_to(ids[:, :size], (8, size)).astype(F32)
    ids_cols = ids_rows.T[:, :1].astype(I32)
    pick = onehot((iota((size, UNIQ), 1) == ids_cols) & valid)
    x = nn(pick, rows)
    unit_in, inv_in = norm_parts(x)
    normed = (unit_in * gin_ref[...]).astype(BF)
    for c in range(4):
        cols = pl.ds(c * D, D)
        half = 0.5 * (nn(normed, win_ref[:, cols]) + bin_ref[:, cols])
        up = 1.0 + jnp.tanh(half)
        act = half * up
        hid[:size, cols] = act.astype(BF)
        slope[:size, cols] = 0.5 * (up + act * (2.0 - up))
    per = jnp.where(valid, 1.0, 0.0) / count.astype(F32)
    blocks = size // 128
    for h in range(HEADS):
        vcol, qcol, kcol = (pl.ds(D * g + h * HEAD, HEAD) for g in (1, 2, 3))
        for bi in range(blocks):
            rs = pl.ds(bi * 128, 128)
            width = (bi + 1) * 128
            if bi == 0:
                bias = bias_ref[h, :128, :]
            else:
                bias = jnp.concatenate([bias_ref[h, 128:, :], bias_ref[h, :128, :]], axis=1)
            half = nt(hid[rs, qcol], hid[:width, kcol]) * (0.5 * SCALE) + bias
            up = 1.0 + jnp.tanh(half)
            act = half * up
            scale = per[bi * 128 : (bi + 1) * 128]
            w = (act * scale).astype(BF)
            wts[h, rs, :width] = w
            wslope[h, rs, :width] = (up + act * (2.0 - up)) * (scale * (0.5 * SCALE))
            mix[rs, pl.ds(h * HEAD, HEAD)] = nn(w, hid[:width, vcol])
    unit_mid, inv_mid = norm_parts(mix[:size, :])
    scaled = unit_mid * gmid_ref[...]
    gate = hid[:size, :D].astype(F32)
    gated = (scaled * gate).astype(BF)
    result = x + nn(gated, wout_ref[...])
    out_ref[0, :size, :] = jnp.where(valid, result, 0.0).astype(BF)
    if size < MAXLEN:
        out_ref[0, size:, :] = jnp.zeros((MAXLEN - size, D), BF)
    grad = jnp.where(valid, cot.astype(F32), 0.0)
    dgated = nt(grad.astype(BF), wout_ref[...]).astype(BF).astype(F32)
    dgate = (dgated * scaled).astype(BF).astype(F32)
    dpre[:size, :D] = (dgate * slope[:size, :D]).astype(BF)
    dmix = norm_grad(dgated * gate * gmid_ref[...], unit_mid, inv_mid).astype(BF)
    for h in range(HEADS):
        vcol, qcol, kcol = (pl.ds(D * g + h * HEAD, HEAD) for g in (1, 2, 3))
        dv = [None] * blocks
        dk = [None] * blocks
        for bi in range(blocks):
            rs = pl.ds(bi * 128, 128)
            width = (bi + 1) * 128
            dm = dmix[bi * 128 : (bi + 1) * 128, h * HEAD : (h + 1) * HEAD]
            dw = nt(dm, hid[:width, vcol])
            ds = (dw * wslope[h, rs, :width]).astype(BF)
            dq = nn(ds, hid[:width, kcol]).astype(BF).astype(F32)
            dpre[rs, qcol] = (dq * slope[rs, qcol]).astype(BF)
            dvs = tn(wts[h, rs, :width], dm)
            dks = tn(ds, hid[rs, qcol])
            for bj in range(bi + 1):
                part = slice(bj * 128, (bj + 1) * 128)
                dv[bj] = dvs[part] if dv[bj] is None else dv[bj] + dvs[part]
                dk[bj] = dks[part] if dk[bj] is None else dk[bj] + dks[part]
        for bj in range(blocks):
            rs = pl.ds(bj * 128, 128)
            dpre[rs, vcol] = (dv[bj].astype(BF).astype(F32) * slope[rs, vcol]).astype(BF)
            dpre[rs, kcol] = (dk[bj].astype(BF).astype(F32) * slope[rs, kcol]).astype(BF)
    dnormed = nt(dpre[:size, :], win_ref[...]).astype(BF).astype(F32)
    dx = norm_grad(dnormed * gin_ref[...], unit_in, inv_in)
    token = (dx + grad).astype(BF)
    back = onehot((iota((UNIQ, size), 0) == ids[:, :size]) & (iota((UNIQ, size), 1) < count))
    sums = nn(back, token)
    acc_ref[...] = jnp.where(fresh, sums, sums + acc_ref[...])


def layer_kernel(plan, aliased, *refs):
    deltas, each = plan
    n_src = len(deltas)
    refs = list(refs)
    seq_ref = refs.pop(0)
    smsg = [refs.pop(0) for _ in range(n_src)]
    vmsg = [refs.pop(0) for _ in range(n_src)]
    rows_refs = [refs.pop(0) for _ in range(n_src)]
    cot_ref = refs.pop(0)
    win_ref, bin_ref, gin_ref, gmid_ref, wout_ref, bias_ref = (refs.pop(0) for _ in range(6))
    if aliased:
        refs.pop(0)
    out_ref = refs.pop(0)
    part_refs = [refs.pop(0) for _ in range(n_src)]
    rows, ids_sc, acc = (refs.pop(0) for _ in range(3))
    scratch = refs
    step = pl.program_id(0)
    src = step // len(each)
    turn = step % len(each)
    count = jnp.int32(0)
    for d in range(n_src):
        for t, b in enumerate(each):
            here = (src == d) & (turn == t)
            count = jnp.where(here, smsg[d][b, MAXLEN], count)

            @pl.when(here)
            def _():
                ids_sc[...] = vmsg[d][b : b + 1, :MAXLEN]
                if t == 0:
                    rows[...] = rows_refs[d][...]

    weights = (win_ref, bin_ref, gin_ref, gmid_ref, wout_ref, bias_ref, *scratch)
    for size in (128, 256):

        @pl.when((count <= 128) == (size == 128))
        def _():
            slot_body(
                size,
                count,
                ids_sc[...],
                rows[...],
                cot_ref[0, :size, :],
                out_ref,
                acc,
                turn == 0,
                weights,
            )

    for d in range(n_src):

        @pl.when((src == d) & (turn == len(each) - 1))
        def _():
            part_refs[d][...] = acc[...].astype(BF)


def layer(plan, seq, msgs, rows, cot, weights, prior):
    deltas, each = plan
    n_src = len(deltas)
    n_each = len(each)

    def slot(i, seq_ref):
        src = i // n_each
        delta = deltas[0]
        for d in range(1, n_src):
            delta = jnp.where(src == d, deltas[d], delta)
        turn = i % n_each
        b = each[0]
        for t in range(1, n_each):
            b = jnp.where(turn == t, each[t], b)
        return ((seq_ref[0] - delta + 4) % 4) * 2 + b, 0, 0

    whole = lambda a: pl.BlockSpec(a.shape, lambda i, s, n=a.ndim: (0,) * n, pipeline_mode=pl.Buffered(1))
    smem = pl.BlockSpec(memory_space=pltpu.SMEM)
    in_specs = [smem] * n_src + [whole(m) for m in msgs] + [whole(r) for r in rows]
    in_specs += [pl.BlockSpec((1, MAXLEN, D), slot)] + [whole(w) for w in weights]
    args = [*msgs, *msgs, *rows, cot, *weights]
    alias = {}
    if prior is not None:
        in_specs.append(pl.BlockSpec(memory_space=pl.ANY))
        args.append(prior)
        alias = {len(args): 0}
    part = jax.ShapeDtypeStruct((UNIQ, D), BF)
    return pl.pallas_call(
        functools.partial(layer_kernel, plan, prior is not None),
        grid_spec=pltpu.PrefetchScalarGridSpec(
            num_scalar_prefetch=1,
            grid=(n_src * n_each,),
            in_specs=in_specs,
            out_specs=[pl.BlockSpec((1, MAXLEN, D), slot)]
            + [pl.BlockSpec((UNIQ, D), lambda i, s: (0, 0))] * n_src,
            scratch_shapes=[
                pltpu.VMEM((UNIQ, D), BF),
                pltpu.VMEM((1, MAXLEN), I32),
                pltpu.VMEM((UNIQ, D), F32),
                pltpu.VMEM((MAXLEN, 4 * D), BF),
                pltpu.VMEM((MAXLEN, 4 * D), F32),
                pltpu.VMEM((HEADS, MAXLEN, MAXLEN), BF),
                pltpu.VMEM((HEADS, MAXLEN, MAXLEN), F32),
                pltpu.VMEM((MAXLEN, 4 * D), BF),
                pltpu.VMEM((MAXLEN, D), F32),
            ],
        ),
        out_shape=[jax.ShapeDtypeStruct(cot.shape, BF)] + [part] * n_src,
        input_output_aliases=alias,
        compiler_params=params(dimension_semantics=("arbitrary",)),
        name="layer",
    )(seq, *args)


def expand_kernel(pos_ref, *refs):
    out_ref = refs[-1]
    total = refs[0][...].astype(F32)
    for r in refs[1:-1]:
        total = total + r[...].astype(F32)
    total = total.astype(BF)
    row = iota((8 * DEVICES, UNIQ), 0)
    pos = pos_ref[...]
    upper = nn(onehot(row == pos), total[:, : D // 2])
    lower = nn(onehot(row == pos + 4), total[:, D // 2 :])
    out_ref[...] = (upper + lower).astype(BF)


def expand(pos, parts):
    return pl.pallas_call(
        expand_kernel,
        out_shape=jax.ShapeDtypeStruct((8 * DEVICES, D // 2), BF),
        compiler_params=params(),
        name="expand",
    )(pos, *parts)


def asked_line_kernel(asked_ref, out_ref):
    parts = []
    spread = onehot(iota((DEVICES, 8 * DEVICES), 0) == (iota((DEVICES, 8 * DEVICES), 1) >> 3))
    for part in asked_parts(asked_ref):
        square = jnp.concatenate([part.astype(F32), jnp.zeros((DEVICES, 124), F32)], axis=1)
        parts.append(nn(square.T[:8].astype(BF), spread))
    value = parts[0] * 32.0 + parts[1]
    mine = iota((8, 8 * DEVICES), 0) == (iota((8, 8 * DEVICES), 1) & 3)
    out_ref[...] = jnp.sum(jnp.where(mine, value, 0.0), axis=0, keepdims=True).astype(I32)


def asked_line(asked):
    return pl.pallas_call(
        asked_line_kernel,
        out_shape=jax.ShapeDtypeStruct((1, 8 * DEVICES), I32),
        compiler_params=params(),
        name="asked_line",
    )(asked)


def scatter_kernel(line_ref, landed_ref, out_ref):
    size = out_ref.shape[0]
    row = iota((size, 8 * DEVICES), 0) + pl.program_id(0) * size
    upper = (iota((1, 8 * DEVICES), 1) & 7) < 4
    line = line_ref[...]
    for half in range(2):
        wanted = jnp.where(upper == (half == 0), line, -1)
        out_ref[:, pl.ds(half * 256, 256)] = nn(onehot(row == wanted), landed_ref[...])


def scatter(line, landed):
    size = 256
    whole = lambda a: pl.BlockSpec(a.shape, lambda i: (0, 0), pipeline_mode=pl.Buffered(1))
    return pl.pallas_call(
        scatter_kernel,
        grid=(ROWS_DEV // size,),
        in_specs=[whole(line), whole(landed)],
        out_specs=pl.BlockSpec((size, D), lambda i: (i, 0)),
        out_shape=jax.ShapeDtypeStruct((ROWS_DEV, D), F32),
        compiler_params=params(dimension_semantics=("arbitrary",)),
        name="scatter",
    )(line, landed)


def ring(delta):
    return [(i, (i + delta) % 4) for i in range(4)]


def exchange(x, shape):
    got = lax.all_to_all(x.reshape(shape), ("emb", "seq"), split_axis=0, concat_axis=0, tiled=True)
    return got.reshape(x.shape)


PLANS = (((0,), (0,)), ((1, 3, 2), (0, 1)), ((0,), (1,)))


def program(
    item_table,
    unique_ids,
    inverse,
    lengths,
    assignment,
    proj_in,
    bias_in,
    gain_in,
    gain_mid,
    proj_out,
    position_bias,
    cotangent,
):
    seq = lax.axis_index("seq").astype(I32).reshape(1)
    req, pos, *sent = pack(assignment, lengths, seq, unique_ids, inverse)
    asked = exchange(req, (DEVICES, 1, 4))
    msgs = [sent[0]] + [lax.ppermute(sent[d], "seq", ring(d)) for d in (1, 2, 3)]
    bias, pos_rows = tables(position_bias, pos)
    answer = answer_rows(asked, item_table)
    got = exchange(answer, (DEVICES, 8, D // 2))
    got, *msgs = lax.optimization_barrier((got, *msgs))
    line = asked_line(asked)
    own = compact(pos_rows, got)
    rows = [own] + [lax.ppermute(own, "seq", ring(d)) for d in (1, 2, 3)]
    weights = (
        proj_in,
        bias_in.reshape(1, 4 * D),
        gain_in.reshape(1, D),
        gain_mid.reshape(1, D),
        proj_out,
        bias,
    )
    outputs = None
    sums = []
    for plan in PLANS:
        outputs, *parts = layer(
            plan,
            seq,
            [msgs[d] for d in plan[0]],
            [rows[d] for d in plan[0]],
            cotangent,
            weights,
            outputs,
        )
        for d, part in zip(plan[0], parts):
            sums.append(part if d == 0 else lax.ppermute(part, "seq", ring(-d)))
    landed = exchange(expand(pos, sums), (DEVICES, 8, D // 2))
    return (outputs, scatter(line, landed))


def solution(mesh):
    both = ("emb", "seq")
    in_specs = (
        P(both, None),
        P(both),
        P(both, None),
        P(both),
        P(both),
        P(),
        P(),
        P(),
        P(),
        P(),
        P(),
        P(both, None, None),
    )
    out_specs = (P(both, None, None), P(both, None))
    return jax.shard_map(program, mesh=mesh, in_specs=in_specs, out_specs=out_specs, check_vma=False)
```

```python
import functools

import jax
import jax.numpy as jnp
from jax import lax
from jax.experimental import pallas as pl
from jax.experimental.pallas import tpu as pltpu
from jax.sharding import PartitionSpec as P

D = 512
HEADS = 4
HEAD = 128
MAXLEN = 256
UNIQ = 256
ROWS_DEV = 1024
DEVICES = 128
SCALE = HEAD**-0.5
EPS = 1e-05
MASKED = -1e30
BF = jnp.bfloat16
F32 = jnp.float32
I32 = jnp.int32


def nn(a, b):
    return lax.dot_general(a, b, (((1,), (0,)), ((), ())), preferred_element_type=F32)


def nt(a, b):
    return lax.dot_general(a, b, (((1,), (1,)), ((), ())), preferred_element_type=F32)


def tn(a, b):
    return lax.dot_general(a, b, (((0,), (0,)), ((), ())), preferred_element_type=F32)


def iota(shape, dim):
    return lax.broadcasted_iota(I32, shape, dim)


def onehot(mask):
    return jnp.where(mask, 1.0, 0.0).astype(BF)


def params(**kw):
    return pltpu.CompilerParams(vmem_limit_bytes=24 << 20, **kw)


def pack_kernel(assign_ref, len_ref, seq_ref, ids_ref, inv_ref, req_ref, pos_ref, *msg_refs):
    ids = ids_ref[...]
    owner = ids >> 10
    local = (ids & (ROWS_DEV - 1)).astype(F32)
    held = iota((DEVICES, UNIQ), 0) == owner
    earlier = onehot(iota((UNIQ, UNIQ), 0) < iota((UNIQ, UNIQ), 1))
    before = nn(onehot(held), earlier)
    rank = jnp.sum(jnp.where(held, before, 0.0), axis=0, keepdims=True)
    pos_ref[...] = owner * 8 + rank.astype(I32)
    lane = iota((DEVICES, 4), 1)
    req = jnp.zeros((DEVICES, 4), F32)
    for r in range(4):
        chosen = held & (before == float(r))
        col = jnp.sum(jnp.where(chosen, ROWS_DEV - local, 0.0), axis=1, keepdims=True)
        req = jnp.where(lane == r, ROWS_DEV - col, req)
    req_ref[...] = req.astype(I32)
    seq = seq_ref[0]
    for j in range(8):
        place = assign_ref[j]
        delta = (place // 8 - seq + 4) % 4
        half = place % 2
        row = jnp.concatenate(
            [inv_ref[j : j + 1, :], jnp.full((1, 128), len_ref[j], I32)], axis=1
        )
        for d in range(4):
            for b in range(2):

                @pl.when((delta == d) & (half == b))
                def _():
                    msg_refs[d][b : b + 1, :] = row


def pack(assignment, lengths, seq, ids, inverse):
    smem = pl.BlockSpec(memory_space=pltpu.SMEM)
    vmem = pl.BlockSpec(memory_space=pltpu.VMEM)
    return pl.pallas_call(
        pack_kernel,
        in_specs=[smem, smem, smem, vmem, vmem],
        out_specs=[vmem] * 6,
        out_shape=[
            jax.ShapeDtypeStruct((DEVICES, 4), I32),
            jax.ShapeDtypeStruct((1, UNIQ), I32),
        ]
        + [jax.ShapeDtypeStruct((2, MAXLEN + 128), I32)] * 4,
        compiler_params=params(),
        name="pack",
    )(assignment, lengths, seq, ids.reshape(1, UNIQ), inverse)


def tables_kernel(flipped_ref, pos_ref, win_ref, wout_ref, bias_ref, pos_rows_ref, winb_ref, woutb_ref):
    i = iota((MAXLEN, MAXLEN), 0)
    j = iota((MAXLEN, MAXLEN), 1)
    for h in range(HEADS):
        line = jnp.broadcast_to(flipped_ref[h : h + 1, :], (MAXLEN, MAXLEN))
        spread = pltpu.roll(line, 1, 1, stride=1, stride_axis=0)
        full = jnp.where(j <= i, 0.5 * spread, MASKED)
        bias_ref[h] = full[:, :128]
    pos = jnp.broadcast_to(pos_ref[...], (UNIQ, UNIQ)).astype(F32)
    col = jnp.sum(jnp.where(i == j, pos, 0.0), axis=1, keepdims=True)
    pos_rows_ref[...] = jnp.broadcast_to(col.astype(I32), (UNIQ, 128))
    for c in range(16):
        winb_ref[c] = win_ref[:, pl.ds(c * 128, 128)]
    for c in range(4):
        woutb_ref[c] = wout_ref[:, pl.ds(c * 128, 128)]


def tables(position_bias, pos, proj_in, proj_out):
    return pl.pallas_call(
        tables_kernel,
        out_shape=[
            jax.ShapeDtypeStruct((HEADS, MAXLEN, 128), F32),
            jax.ShapeDtypeStruct((UNIQ, 128), I32),
            jax.ShapeDtypeStruct((16, D, 128), BF),
            jax.ShapeDtypeStruct((4, D, 128), BF),
        ],
        compiler_params=params(),
        name="tables",
    )(position_bias[:, ::-1], pos, proj_in, proj_out)


def asked_parts(asked_ref):
    asked = asked_ref[...]
    return (asked >> 5).astype(BF), (asked & 31).astype(BF)


def answer_kernel(asked_ref, table_ref, out_ref):
    high, low = asked_parts(asked_ref)
    count = 256
    for c in range(8 * DEVICES // count):
        row = iota((count, DEVICES), 0) + c * count
        spread = onehot((row >> 3) == iota((count, DEVICES), 1))
        value = nn(spread, high) * 32.0 + nn(spread, low)
        rank = (iota((count, 4), 0)) & 3
        col = jnp.sum(jnp.where(iota((count, 4), 1) == rank, value, 0.0), axis=1, keepdims=True)
        pick = onehot(iota((count, ROWS_DEV), 1) == col.astype(I32))
        both = nn(pick, table_ref[...])
        upper = (iota((count, D // 2), 0) & 7) < 4
        out_ref[pl.ds(c * count, count), :] = jnp.where(
            upper, both[:, : D // 2], both[:, D // 2 :]
        ).astype(BF)


def answer_rows(asked, table):
    return pl.pallas_call(
        answer_kernel,
        out_shape=jax.ShapeDtypeStruct((8 * DEVICES, D // 2), BF),
        compiler_params=params(),
        name="answer",
    )(asked, table)


def compact_kernel(pos_ref, got_ref, out_ref):
    pos = pos_ref[:, :1]
    lane = iota((UNIQ, 8 * DEVICES), 1)
    for half in range(2):
        pick = onehot(lane == pos + 4 * half)
        out_ref[:, pl.ds(half * 256, 256)] = nn(pick, got_ref[...]).astype(BF)


def compact(pos_rows, got):
    return pl.pallas_call(
        compact_kernel,
        out_shape=jax.ShapeDtypeStruct((UNIQ, D), BF),
        compiler_params=params(),
        name="compact",
    )(pos_rows, got)


def row_mean(x):
    return jnp.sum(x, axis=-1, keepdims=True) * (1.0 / D)


def norm_parts(x):
    center = x - row_mean(x)
    spread = row_mean(center * center)
    inv = lax.rsqrt(spread + EPS)
    return center * inv, inv


def norm_grad(g, unit, inv):
    return inv * (g - row_mean(g) - unit * row_mean(g * unit))


def chunks(size, step=64):
    return [slice(r, r + step) for r in range(0, size, step)]


def side(ref, first, count, rs=slice(None)):
    return jnp.concatenate([ref[c, rs] for c in range(first, first + count)], axis=1)


def lay(ref, rs, value):
    for c in range(value.shape[1] // 128):
        ref[c, rs] = value[:, c * 128 : (c + 1) * 128].astype(BF)


def rows_body(segments, ids_of, rows, cot_ref, out_ref, acc_ref, fresh, refs):
    (win_ref, bin_ref, gin_ref, gmid_ref, wout_ref, bias_ref) = refs[:6]
    (hid, slope, wts, wslope, dpre, xs, unit_in, unit_mid, invs, narrow, wide) = refs[6:]
    size = sum(seg[1] for seg in segments)
    every = slice(0, size)
    gin_half = 0.5 * gin_ref[...]
    lines = []
    for first, length, count, place in segments:
        line = ids_of(place)[:, :length]
        lines.append(jnp.where(iota((1, length), 1) < count, line, -1))
    line = lines[0] if len(lines) == 1 else jnp.concatenate(lines, axis=1)
    cols = jnp.broadcast_to(line, (8, size)).astype(F32).T[:, :1].astype(I32)
    xs[:size] = nn(onehot(iota((size, UNIQ), 1) == cols), rows)
    for rs in chunks(size):
        unit, inv = norm_parts(xs[rs])
        unit_in[rs] = unit
        invs[rs] = jnp.broadcast_to(inv, (rs.stop - rs.start, 128))
        lay(narrow, rs, unit * gin_half)
    for c in (6, 7, 4, 5, 2, 3, 0, 1):
        pre = nn(side(narrow, 0, 4, every), side(win_ref, 2 * c, 2))
        for k in range(2):
            blk = 2 * c + k
            half = pre[:, k * 128 : (k + 1) * 128] + 0.5 * bin_ref[:, pl.ds(blk * 128, 128)]
            up = 1.0 + jnp.tanh(half)
            act = half * up
            hid[blk, every] = act.astype(BF)
            slope[blk, every] = (up + act * (2.0 - up)).astype(BF)
    units = []
    for h in range(HEADS):
        for first, length, count, place in segments:
            for bi in range(length // 128):
                units.append((h, first, bi, count))
    for h, first, bi, count in units:
        rs = slice(first + bi * 128, first + bi * 128 + 128)
        per = jnp.where(
            iota((128, 1), 0) + bi * 128 < count,
            1.0 / jnp.full((1, 1), count, I32).astype(F32),
            0.0,
        )
        for bj in range(bi + 1):
            ks = slice(first + bj * 128, first + bj * 128 + 128)
            bias = bias_ref[h, (bi - bj) * 128 : (bi - bj) * 128 + 128, :]
            half = nt(hid[8 + h, rs], hid[12 + h, ks]) * (0.5 * SCALE) + bias
            up = 1.0 + jnp.tanh(half)
            act = half * up
            wts[h, bj, rs] = (act * per).astype(BF)
            wslope[h, bj, rs] = ((up + act * (2.0 - up)) * (per * (0.5 * SCALE))).astype(BF)
    for h, first, bi, count in units:
        rs = slice(first + bi * 128, first + bi * 128 + 128)
        ks = slice(first, first + (bi + 1) * 128)
        wide[rs, pl.ds(h * HEAD, HEAD)] = nn(side(wts.at[h], 0, bi + 1, rs), hid[4 + h, ks])
    for rs in chunks(size):
        unit, inv = norm_parts(wide[rs])
        unit_mid[rs] = unit
        lay(narrow, rs, unit * gmid_ref[...] * side(hid, 0, 4, rs).astype(F32))
        wide[rs, :128] = jnp.broadcast_to(inv, (rs.stop - rs.start, 128))
    result = nn(side(narrow, 0, 4, every), side(wout_ref, 0, 4))
    for first, length, count, place in segments:
        valid = iota((length, 1), 0) < count
        rs = slice(first, first + length)
        out_ref[place, :length, :] = jnp.where(valid, xs[rs] + result[rs], 0.0).astype(BF)
        if length < MAXLEN:
            out_ref[place, length:, :] = jnp.zeros((MAXLEN - length, D), BF)
        lay(narrow, rs, jnp.where(valid, cot_ref[place, :length, :], jnp.zeros((), BF)))
    xs[:size] = nt(side(narrow, 0, 4, every), side(wout_ref, 0, 4))
    for rs in chunks(size):
        unit = unit_mid[rs]
        inv = wide[rs, :1]
        grown = xs[rs] * gmid_ref[...]
        scaled = grown * unit
        for c in range(4):
            dpre[c, rs] = scaled[:, c * 128 : (c + 1) * 128].astype(BF) * slope[c, rs]
        lay(hid, rs, norm_grad(grown * side(hid, 0, 4, rs).astype(F32), unit, inv))
    for h, first, bi, count in units:
        rs = slice(first + bi * 128, first + bi * 128 + 128)
        for bj in range(bi + 1):
            ks = slice(first + bj * 128, first + bj * 128 + 128)
            wslope[h, bj, rs] = nt(hid[h, rs], hid[4 + h, ks]).astype(BF) * wslope[h, bj, rs]
    for h, first, bi, count in units:
        rs = slice(first + bi * 128, first + bi * 128 + 128)
        ks = slice(first, first + (bi + 1) * 128)
        dq = nn(side(wslope.at[h], 0, bi + 1, rs), hid[12 + h, ks])
        dpre[8 + h, rs] = dq.astype(BF) * slope[8 + h, rs]
    for h in range(HEADS):
        for first, length, count, place in segments:
            for bj in range(length // 128):
                ks = slice(first + bj * 128, first + bj * 128 + 128)
                qs = slice(first + bj * 128, first + length)
                dv = tn(wts[h, bj, qs], hid[h, qs])
                dpre[4 + h, ks] = dv.astype(BF) * slope[4 + h, ks]
                dk = tn(wslope[h, bj, qs], hid[8 + h, qs])
                dpre[12 + h, ks] = dk.astype(BF) * slope[12 + h, ks]
    wide[:size] = nt(side(dpre, 0, 16, every), side(win_ref, 0, 16))
    for rs in chunks(size):
        dx = norm_grad(wide[rs] * gin_half, unit_in[rs], invs[rs, :1])
        lay(narrow, rs, dx + side(narrow, 0, 4, rs).astype(F32))
    sums = nn(onehot(iota((UNIQ, size), 0) == line), side(narrow, 0, 4, every))
    acc_ref[...] = jnp.where(fresh, sums, sums + acc_ref[...])


def layer_kernel(plan, aliased, *refs):
    deltas, each = plan
    n_src = len(deltas)
    n_each = len(each)
    refs = list(refs)
    refs.pop(0)
    smsg = [refs.pop(0) for _ in range(n_src)]
    vmsg = [refs.pop(0) for _ in range(n_src)]
    rows_refs = [refs.pop(0) for _ in range(n_src)]
    cot_ref = refs.pop(0)
    weights = [refs.pop(0) for _ in range(6)]
    if aliased:
        refs.pop(0)
    out_ref = refs.pop(0)
    part_refs = [refs.pop(0) for _ in range(n_src)]
    rows, ids_sc, acc = (refs.pop(0) for _ in range(3))
    work = (*weights, *refs)
    src = pl.program_id(0)
    counts = []
    for b in each:
        count = smsg[0][b, MAXLEN]
        for d in range(1, n_src):
            count = jnp.where(src == d, smsg[d][b, MAXLEN], count)
        counts.append(count)
    for d in range(n_src):

        @pl.when(src == d)
        def _():
            for t, b in enumerate(each):
                ids_sc[t : t + 1, :] = vmsg[d][b : b + 1, :MAXLEN]
            rows[...] = rows_refs[d][...]

    def ids_of(place):
        return ids_sc[pl.ds(place, 1), :]

    def run(segments, fresh):
        rows_body(segments, ids_of, rows[...], cot_ref, out_ref, acc, fresh, work)

    def alone(place, count, fresh):
        for size in (128, 256):

            @pl.when((count <= 128) == (size == 128))
            def _():
                run([(0, size, count, place)], fresh)

    if n_each == 1:
        alone(0, counts[0], True)
    else:
        short = (counts[0] <= 128) & (counts[1] <= 128)

        @pl.when(short)
        def _():
            run([(0, 128, counts[0], 0), (128, 128, counts[1], 1)], True)

        @pl.when(jnp.logical_not(short))
        def _():
            def one(t, carry):
                alone(t, jnp.where(t == 0, counts[0], counts[1]), t == 0)
                return carry

            lax.fori_loop(0, 2, one, 0)

    for d in range(n_src):

        @pl.when(src == d)
        def _():
            part_refs[d][...] = acc[...].astype(BF)


def layer(plan, seq, msgs, rows, cot, weights, prior):
    deltas, each = plan
    n_src = len(deltas)
    n_each = len(each)

    def slot(i, seq_ref):
        delta = deltas[0]
        for d in range(1, n_src):
            delta = jnp.where(i == d, deltas[d], delta)
        source = (seq_ref[0] - delta + 4) % 4
        return (source if n_each == 2 else source * 2 + each[0]), 0, 0

    whole = lambda a: pl.BlockSpec(a.shape, lambda i, s, n=a.ndim: (0,) * n, pipeline_mode=pl.Buffered(1))
    smem = pl.BlockSpec(memory_space=pltpu.SMEM)
    in_specs = [smem] * n_src + [whole(m) for m in msgs] + [whole(r) for r in rows]
    in_specs += [pl.BlockSpec((n_each, MAXLEN, D), slot)] + [whole(w) for w in weights]
    args = [*msgs, *msgs, *rows, cot, *weights]
    alias = {}
    if prior is not None:
        in_specs.append(pl.BlockSpec(memory_space=pl.ANY))
        args.append(prior)
        alias = {len(args): 0}
    part = jax.ShapeDtypeStruct((UNIQ, D), BF)
    return pl.pallas_call(
        functools.partial(layer_kernel, plan, prior is not None),
        grid_spec=pltpu.PrefetchScalarGridSpec(
            num_scalar_prefetch=1,
            grid=(n_src,),
            in_specs=in_specs,
            out_specs=[pl.BlockSpec((n_each, MAXLEN, D), slot)]
            + [pl.BlockSpec((UNIQ, D), lambda i, s: (0, 0))] * n_src,
            scratch_shapes=[
                pltpu.VMEM((UNIQ, D), BF),
                pltpu.VMEM((8, MAXLEN), I32),
                pltpu.VMEM((UNIQ, D), F32),
                pltpu.VMEM((16, MAXLEN, 128), BF),
                pltpu.VMEM((16, MAXLEN, 128), BF),
                pltpu.VMEM((HEADS, 2, MAXLEN, 128), BF),
                pltpu.VMEM((HEADS, 2, MAXLEN, 128), BF),
                pltpu.VMEM((16, MAXLEN, 128), BF),
                pltpu.VMEM((MAXLEN, D), F32),
                pltpu.VMEM((MAXLEN, D), F32),
                pltpu.VMEM((MAXLEN, D), F32),
                pltpu.VMEM((MAXLEN, 128), F32),
                pltpu.VMEM((4, MAXLEN, 128), BF),
                pltpu.VMEM((MAXLEN, D), F32),
            ],
        ),
        out_shape=[jax.ShapeDtypeStruct(cot.shape, BF)] + [part] * n_src,
        input_output_aliases=alias,
        compiler_params=params(dimension_semantics=("arbitrary",)),
        name="layer",
    )(seq, *args)


def expand_kernel(pos_ref, *refs):
    out_ref = refs[-1]
    total = refs[0][...].astype(F32)
    for r in refs[1:-1]:
        total = total + r[...].astype(F32)
    total = total.astype(BF)
    row = iota((8 * DEVICES, UNIQ), 0)
    pos = pos_ref[...]
    upper = nn(onehot(row == pos), total[:, : D // 2])
    lower = nn(onehot(row == pos + 4), total[:, D // 2 :])
    out_ref[...] = (upper + lower).astype(BF)


def expand(pos, parts):
    return pl.pallas_call(
        expand_kernel,
        out_shape=jax.ShapeDtypeStruct((8 * DEVICES, D // 2), BF),
        compiler_params=params(),
        name="expand",
    )(pos, *parts)


def asked_line_kernel(asked_ref, out_ref):
    parts = []
    spread = onehot(iota((DEVICES, 8 * DEVICES), 0) == (iota((DEVICES, 8 * DEVICES), 1) >> 3))
    for part in asked_parts(asked_ref):
        square = jnp.concatenate([part.astype(F32), jnp.zeros((DEVICES, 124), F32)], axis=1)
        parts.append(nn(square.T[:8].astype(BF), spread))
    value = parts[0] * 32.0 + parts[1]
    mine = iota((8, 8 * DEVICES), 0) == (iota((8, 8 * DEVICES), 1) & 3)
    out_ref[...] = jnp.sum(jnp.where(mine, value, 0.0), axis=0, keepdims=True).astype(I32)


def asked_line(asked):
    return pl.pallas_call(
        asked_line_kernel,
        out_shape=jax.ShapeDtypeStruct((1, 8 * DEVICES), I32),
        compiler_params=params(),
        name="asked_line",
    )(asked)


def scatter_kernel(line_ref, landed_ref, out_ref):
    size = out_ref.shape[0]
    row = iota((size, 8 * DEVICES), 0) + pl.program_id(0) * size
    upper = (iota((1, 8 * DEVICES), 1) & 7) < 4
    line = line_ref[...]
    for half in range(2):
        wanted = jnp.where(upper == (half == 0), line, -1)
        out_ref[:, pl.ds(half * 256, 256)] = nn(onehot(row == wanted), landed_ref[...])


def scatter(line, landed):
    size = 256
    whole = lambda a: pl.BlockSpec(a.shape, lambda i: (0, 0), pipeline_mode=pl.Buffered(1))
    return pl.pallas_call(
        scatter_kernel,
        grid=(ROWS_DEV // size,),
        in_specs=[whole(line), whole(landed)],
        out_specs=pl.BlockSpec((size, D), lambda i: (i, 0)),
        out_shape=jax.ShapeDtypeStruct((ROWS_DEV, D), F32),
        compiler_params=params(dimension_semantics=("arbitrary",)),
        name="scatter",
    )(line, landed)


def ring(delta):
    return [(i, (i + delta) % 4) for i in range(4)]


def exchange(x, shape):
    got = lax.all_to_all(x.reshape(shape), ("emb", "seq"), split_axis=0, concat_axis=0, tiled=True)
    return got.reshape(x.shape)


PLANS = (((0,), (0,)), ((1, 3, 2), (0, 1)), ((0,), (1,)))


def program(
    item_table,
    unique_ids,
    inverse,
    lengths,
    assignment,
    proj_in,
    bias_in,
    gain_in,
    gain_mid,
    proj_out,
    position_bias,
    cotangent,
):
    seq = lax.axis_index("seq").astype(I32).reshape(1)
    req, pos, *sent = pack(assignment, lengths, seq, unique_ids, inverse)
    asked = exchange(req, (DEVICES, 1, 4))
    msgs = [sent[0]] + [lax.ppermute(sent[d], "seq", ring(d)) for d in (1, 2, 3)]
    bias, pos_rows, win, wout = tables(position_bias, pos, proj_in, proj_out)
    answer = answer_rows(asked, item_table)
    got = exchange(answer, (DEVICES, 8, D // 2))
    got, *msgs = lax.optimization_barrier((got, *msgs))
    line = asked_line(asked)
    own = compact(pos_rows, got)
    rows = [own] + [lax.ppermute(own, "seq", ring(d)) for d in (1, 2, 3)]
    weights = (
        win,
        bias_in.reshape(1, 4 * D),
        gain_in.reshape(1, D),
        gain_mid.reshape(1, D),
        wout,
        bias,
    )
    outputs = None
    sums = []
    for plan in PLANS:
        outputs, *parts = layer(
            plan,
            seq,
            [msgs[d] for d in plan[0]],
            [rows[d] for d in plan[0]],
            cotangent,
            weights,
            outputs,
        )
        for d, part in zip(plan[0], parts):
            sums.append(part if d == 0 else lax.ppermute(part, "seq", ring(-d)))
    landed = exchange(expand(pos, sums), (DEVICES, 8, D // 2))
    return (outputs, scatter(line, landed))


def solution(mesh):
    both = ("emb", "seq")
    in_specs = (
        P(both, None),
        P(both),
        P(both, None),
        P(both),
        P(both),
        P(),
        P(),
        P(),
        P(),
        P(),
        P(),
        P(both, None, None),
    )
    out_specs = (P(both, None, None), P(both, None))
    return jax.shard_map(program, mesh=mesh, in_specs=in_specs, out_specs=out_specs, check_vma=False)
```

```python
import functools

import jax
import jax.numpy as jnp
from jax import lax
from jax.experimental import pallas as pl
from jax.experimental.pallas import tpu as pltpu
from jax.sharding import PartitionSpec as P

D = 512
HEADS = 4
HEAD = 128
MAXLEN = 256
UNIQ = 256
ROWS_DEV = 1024
DEVICES = 128
SCALE = HEAD**-0.5
EPS = 1e-05
MASKED = -1e30
BF = jnp.bfloat16
F32 = jnp.float32
I32 = jnp.int32


def nn(a, b):
    return lax.dot_general(a, b, (((1,), (0,)), ((), ())), preferred_element_type=F32)


def nt(a, b):
    return lax.dot_general(a, b, (((1,), (1,)), ((), ())), preferred_element_type=F32)


def tn(a, b):
    return lax.dot_general(a, b, (((0,), (0,)), ((), ())), preferred_element_type=F32)


def iota(shape, dim):
    return lax.broadcasted_iota(I32, shape, dim)


def onehot(mask):
    return jnp.where(mask, 1.0, 0.0).astype(BF)


def in_hbm(x):
    return pltpu.with_memory_space_constraint(x, pltpu.HBM)


def params(**kw):
    return pltpu.CompilerParams(vmem_limit_bytes=24 << 20, **kw)


def pack_kernel(assign_hbm, len_hbm, seq_ref, ids_hbm, inv_hbm, req_ref, pos_ref, *refs):
    msg_refs = refs[:4]
    assign_ref, len_ref, ids_ref, inv_ref, sems = refs[4:]
    loads = [
        pltpu.make_async_copy(src, dst, sems.at[k])
        for k, (src, dst) in enumerate(
            (
                (ids_hbm, ids_ref),
                (inv_hbm, inv_ref),
                (assign_hbm, assign_ref),
                (len_hbm, len_ref),
            )
        )
    ]
    for load in loads:
        load.start()
    loads[0].wait()
    ids = ids_ref[...]
    owner = ids >> 10
    local = (ids & (ROWS_DEV - 1)).astype(F32)
    held = iota((DEVICES, UNIQ), 0) == owner
    earlier = onehot(iota((UNIQ, UNIQ), 0) < iota((UNIQ, UNIQ), 1))
    before = nn(onehot(held), earlier)
    rank = jnp.sum(jnp.where(held, before, 0.0), axis=0, keepdims=True)
    pos_ref[...] = owner * 8 + rank.astype(I32)
    lane = iota((DEVICES, 4), 1)
    req = jnp.zeros((DEVICES, 4), F32)
    for r in range(4):
        chosen = held & (before == float(r))
        col = jnp.sum(jnp.where(chosen, ROWS_DEV - local, 0.0), axis=1, keepdims=True)
        req = jnp.where(lane == r, ROWS_DEV - col, req)
    req_ref[...] = req.astype(I32)
    for load in loads[1:]:
        load.wait()
    seq = seq_ref[0]
    for j in range(8):
        place = assign_ref[j]
        delta = (place // 8 - seq + 4) % 4
        half = place % 2
        row = jnp.concatenate(
            [inv_ref[j : j + 1, :], jnp.full((1, 128), len_ref[j], I32)], axis=1
        )
        for d in range(4):
            for b in range(2):

                @pl.when((delta == d) & (half == b))
                def _():
                    msg_refs[d][b : b + 1, :] = row


def pack(assignment, lengths, seq, ids, inverse):
    smem = pl.BlockSpec(memory_space=pltpu.SMEM)
    vmem = pl.BlockSpec(memory_space=pltpu.VMEM)
    hbm = pl.BlockSpec(memory_space=pltpu.HBM)
    return pl.pallas_call(
        pack_kernel,
        in_specs=[hbm, hbm, smem, hbm, hbm],
        scratch_shapes=[
            pltpu.SMEM((8,), I32),
            pltpu.SMEM((8,), I32),
            pltpu.VMEM((1, UNIQ), I32),
            pltpu.VMEM((8, MAXLEN), I32),
            pltpu.SemaphoreType.DMA((4,)),
        ],
        out_specs=[vmem] * 6,
        out_shape=[
            jax.ShapeDtypeStruct((DEVICES, 4), I32),
            jax.ShapeDtypeStruct((1, UNIQ), I32),
        ]
        + [jax.ShapeDtypeStruct((2, MAXLEN + 128), I32)] * 4,
        compiler_params=params(),
        name="pack",
    )(in_hbm(assignment), in_hbm(lengths), seq, in_hbm(ids.reshape(1, UNIQ)), in_hbm(inverse))


def tables_kernel(flipped_ref, pos_ref, win_hbm, wout_hbm, *refs):
    bias_ref, pos_rows_ref, winb_hbm, woutb_hbm, win_ref, wout_ref, winb_ref, woutb_ref, sems = refs
    loads = [
        pltpu.make_async_copy(win_hbm, win_ref, sems.at[0]),
        pltpu.make_async_copy(wout_hbm, wout_ref, sems.at[1]),
    ]
    stores = [
        pltpu.make_async_copy(winb_ref, winb_hbm, sems.at[2]),
        pltpu.make_async_copy(woutb_ref, woutb_hbm, sems.at[3]),
    ]
    for load in loads:
        load.start()
    i = iota((MAXLEN, MAXLEN), 0)
    j = iota((MAXLEN, MAXLEN), 1)
    for h in range(HEADS):
        line = jnp.broadcast_to(flipped_ref[h : h + 1, :], (MAXLEN, MAXLEN))
        spread = pltpu.roll(line, 1, 1, stride=1, stride_axis=0)
        full = jnp.where(j <= i, 0.5 * spread, MASKED)
        bias_ref[h] = full[:, :128]
    pos = jnp.broadcast_to(pos_ref[...], (UNIQ, UNIQ)).astype(F32)
    col = jnp.sum(jnp.where(i == j, pos, 0.0), axis=1, keepdims=True)
    pos_rows_ref[...] = jnp.broadcast_to(col.astype(I32), (UNIQ, 128))
    for load, store, src, dst in zip(loads, stores, (win_ref, wout_ref), (winb_ref, woutb_ref)):
        load.wait()
        for c in range(dst.shape[0]):
            dst[c] = src[:, pl.ds(c * 128, 128)]
        store.start()
    for store in stores:
        store.wait()


def tables(position_bias, pos, proj_in, proj_out):
    vmem = pl.BlockSpec(memory_space=pltpu.VMEM)
    hbm = pl.BlockSpec(memory_space=pltpu.HBM)
    return pl.pallas_call(
        tables_kernel,
        out_shape=[
            jax.ShapeDtypeStruct((HEADS, MAXLEN, 128), F32),
            jax.ShapeDtypeStruct((UNIQ, 128), I32),
            pltpu.HBM((16, D, 128), BF),
            pltpu.HBM((4, D, 128), BF),
        ],
        in_specs=[vmem, vmem, hbm, hbm],
        out_specs=[vmem, vmem, hbm, hbm],
        scratch_shapes=[
            pltpu.VMEM((D, 4 * D), BF),
            pltpu.VMEM((D, D), BF),
            pltpu.VMEM((16, D, 128), BF),
            pltpu.VMEM((4, D, 128), BF),
            pltpu.SemaphoreType.DMA((4,)),
        ],
        compiler_params=params(),
        name="tables",
    )(position_bias[:, ::-1], pos, in_hbm(proj_in), in_hbm(proj_out))


def asked_parts(asked_ref):
    asked = asked_ref[...]
    return (asked >> 5).astype(BF), (asked & 31).astype(BF)


def to_halves(x):
    groups = x.shape[0] // 8
    upper = iota((groups, 8, D // 2), 1) < 4
    low = x[:, : D // 2].reshape(groups, 8, D // 2)
    high = x[:, D // 2 :].reshape(groups, 8, D // 2)
    even = jnp.where(upper, low, pltpu.roll(high, 4, 1))
    odd = jnp.where(upper, pltpu.roll(low, 4, 1), high)
    both = jnp.concatenate([even[:, None], odd[:, None]], axis=1)
    return both.reshape(groups * 16, D // 2)


def from_halves(x):
    groups = x.shape[0] // 16
    upper = iota((groups, 8, D // 2), 1) < 4
    pairs = x.reshape(groups, 2, 8, D // 2)
    even = pairs[:, 0]
    odd = pairs[:, 1]
    low = jnp.where(upper, even, pltpu.roll(odd, 4, 1))
    high = jnp.where(upper, pltpu.roll(even, 4, 1), odd)
    flat = (groups * 8, D // 2)
    return jnp.concatenate([low.reshape(flat), high.reshape(flat)], axis=1)


def answer_kernel(asked_ref, table_hbm, out_ref, table_ref, pick_ref, sem):
    load = pltpu.make_async_copy(table_hbm, table_ref, sem.at[0])
    load.start()
    high, low = asked_parts(asked_ref)
    count = 4 * DEVICES
    spread = onehot((iota((count, DEVICES), 0) >> 2) == iota((count, DEVICES), 1))
    value = nn(spread, high) * 32.0 + nn(spread, low)
    mine = iota((count, 4), 1) == (iota((count, 4), 0) & 3)
    col = jnp.sum(jnp.where(mine, value, 0.0), axis=1, keepdims=True).astype(I32)
    pick_ref[...] = onehot(iota((count, ROWS_DEV), 1) == col)
    load.wait()
    for c in range(2):
        rows = nn(pick_ref[pl.ds(c * 256, 256), :], table_ref[...])
        out_ref[pl.ds(c * 512, 512), :] = to_halves(rows).astype(BF)


def answer_rows(asked, table):
    return pl.pallas_call(
        answer_kernel,
        in_specs=[pl.BlockSpec(memory_space=pltpu.VMEM), pl.BlockSpec(memory_space=pltpu.HBM)],
        out_shape=jax.ShapeDtypeStruct((8 * DEVICES, D // 2), BF),
        scratch_shapes=[
            pltpu.VMEM((ROWS_DEV, D), BF),
            pltpu.VMEM((4 * DEVICES, ROWS_DEV), BF),
            pltpu.SemaphoreType.DMA((1,)),
        ],
        compiler_params=params(),
        name="answer",
    )(asked, in_hbm(table))


def compact_kernel(pos_ref, got_ref, out_ref):
    pos = pos_ref[:, :1]
    lane = iota((UNIQ, 8 * DEVICES), 1)
    for half in range(2):
        pick = onehot(lane == pos + 4 * half)
        out_ref[:, pl.ds(half * 256, 256)] = nn(pick, got_ref[...]).astype(BF)


def compact(pos_rows, got):
    return pl.pallas_call(
        compact_kernel,
        out_shape=jax.ShapeDtypeStruct((UNIQ, D), BF),
        compiler_params=params(),
        name="compact",
    )(pos_rows, got)


def row_mean(x):
    return jnp.sum(x, axis=-1, keepdims=True) * (1.0 / D)


def norm_parts(x):
    center = x - row_mean(x)
    spread = row_mean(center * center)
    inv = lax.rsqrt(spread + EPS)
    return center * inv, inv


def norm_grad(g, unit, inv):
    return inv * (g - row_mean(g) - unit * row_mean(g * unit))


def chunks(size, step=64):
    return [slice(r, r + step) for r in range(0, size, step)]


def side(ref, first, count, rs=slice(None)):
    return jnp.concatenate([ref[c, rs] for c in range(first, first + count)], axis=1)


def lay(ref, rs, value):
    for c in range(value.shape[1] // 128):
        ref[c, rs] = value[:, c * 128 : (c + 1) * 128].astype(BF)


ORDER = (6, 7, 4, 5, 2, 3, 0, 1)


def rows_body(long, one, two, counts, msg, rows, cot_ref, stage_ref, send, ready, acc_ref, fresh, refs):
    (win_ref, bin_ref, gin_ref, gmid_ref, wout_ref, bias_ref) = refs[:6]
    (hid, slope, wts, wslope, dpre, xs, unit_in, unit_mid, invs, narrow, wide) = refs[6:]
    size = MAXLEN
    every = slice(0, size)
    firsts, seconds = slice(0, 128), slice(128, 256)
    gin_half = 0.5 * gin_ref[...]
    start = jnp.where(long, 128, 0)
    lane = iota((1, 128), 1)
    ids_one, ids_two = msg
    line = jnp.concatenate(
        [
            jnp.where(lane < counts[0], ids_one[:, :128], -1),
            jnp.where(lane + start < counts[1], jnp.where(long, ids_one[:, 128:], ids_two[:, :128]), -1),
        ],
        axis=1,
    )
    cols = jnp.broadcast_to(line, (8, size)).astype(F32).T[:, :1].astype(I32)
    xs[...] = nn(onehot(iota((size, UNIQ), 1) == cols), rows)
    for rs in chunks(size):
        unit, inv = norm_parts(xs[rs])
        unit_in[rs] = unit
        invs[rs] = jnp.broadcast_to(inv, (rs.stop - rs.start, 128))
        lay(narrow, rs, unit * gin_half)
    for c in ORDER:
        ready(c)
        pre = nn(side(narrow, 0, 4, every), side(win_ref, 2 * c, 2))
        for k in range(2):
            blk = 2 * c + k
            half = pre[:, k * 128 : (k + 1) * 128] + 0.5 * bin_ref[:, pl.ds(blk * 128, 128)]
            up = 1.0 + jnp.tanh(half)
            act = half * up
            hid[blk] = act.astype(BF)
            slope[blk] = (up + act * (2.0 - up)).astype(BF)
    valid = [iota((128, 1), 0) < counts[0], iota((128, 1), 0) + start < counts[1]]
    per = []
    for part in range(2):
        inverse = 1.0 / jnp.full((1, 1), jnp.maximum(counts[part], 1), I32).astype(F32)
        per.append(jnp.where(valid[part], inverse, 0.0))
    cross = per[1] * jnp.where(long, 1.0, 0.0)
    blocks = ((0, 0, per[0]), (1, 1, per[1]), (1, 0, cross))
    cut = lambda i: slice(i * 128, i * 128 + 128)
    for h in range(HEADS):
        for bi, bj, scale in blocks:
            bias = bias_ref[h, (bi - bj) * 128 : (bi - bj) * 128 + 128, :]
            half = nt(hid[8 + h, cut(bi)], hid[12 + h, cut(bj)]) * (0.5 * SCALE) + bias
            up = 1.0 + jnp.tanh(half)
            act = half * up
            wts[h, bj, cut(bi)] = (act * scale).astype(BF)
            wslope[h, bj, cut(bi)] = ((up + act * (2.0 - up)) * (scale * (0.5 * SCALE))).astype(BF)
    for h in range(HEADS):
        for bi in range(2):
            wide[cut(bi), pl.ds(h * HEAD, HEAD)] = nn(
                side(wts.at[h], 0, bi + 1, cut(bi)), hid[4 + h, : (bi + 1) * 128]
            )
    for rs in chunks(size):
        unit, inv = norm_parts(wide[rs])
        unit_mid[rs] = unit
        lay(narrow, rs, unit * gmid_ref[...] * side(hid, 0, 4, rs).astype(F32))
        wide[rs, :128] = jnp.broadcast_to(inv, (rs.stop - rs.start, 128))
    ready(8)
    result = nn(side(narrow, 0, 4, every), side(wout_ref, 0, 4))
    other = jnp.where(long, one, two)
    for half, rs in enumerate((firsts, seconds)):
        stage_ref[rs] = jnp.where(valid[half], xs[rs] + result[rs], 0.0).astype(BF)
    send(one, 0, 0)
    send(other, pl.multiple_of(start, 128), 1)
    zero = jnp.zeros((), BF)
    lay(narrow, firsts, jnp.where(valid[0], cot_ref[one, :128, :], zero))
    lay(
        narrow,
        seconds,
        jnp.where(valid[1], cot_ref[other, pl.ds(pl.multiple_of(start, 128), 128), :], zero),
    )
    xs[...] = nt(side(narrow, 0, 4, every), side(wout_ref, 0, 4))
    for rs in chunks(size):
        unit = unit_mid[rs]
        inv = wide[rs, :1]
        grown = xs[rs] * gmid_ref[...]
        scaled = grown * unit
        for c in range(4):
            dpre[c, rs] = scaled[:, c * 128 : (c + 1) * 128].astype(BF) * slope[c, rs]
        lay(hid, rs, norm_grad(grown * side(hid, 0, 4, rs).astype(F32), unit, inv))
    for h in range(HEADS):
        for bi, bj, scale in blocks:
            ds = nt(hid[h, cut(bi)], hid[4 + h, cut(bj)]).astype(BF)
            wslope[h, bj, cut(bi)] = ds * wslope[h, bj, cut(bi)]
    for h in range(HEADS):
        for bi in range(2):
            dq = nn(side(wslope.at[h], 0, bi + 1, cut(bi)), hid[12 + h, : (bi + 1) * 128])
            dpre[8 + h, cut(bi)] = dq.astype(BF) * slope[8 + h, cut(bi)]
    for h in range(HEADS):
        for bj in range(2):
            qs = slice(bj * 128, size)
            dv = tn(wts[h, bj, qs], hid[h, qs])
            dpre[4 + h, cut(bj)] = dv.astype(BF) * slope[4 + h, cut(bj)]
            dk = tn(wslope[h, bj, qs], hid[8 + h, qs])
            dpre[12 + h, cut(bj)] = dk.astype(BF) * slope[12 + h, cut(bj)]
    wide[...] = nt(side(dpre, 0, 16, every), side(win_ref, 0, 16))
    for rs in chunks(size):
        dx = norm_grad(wide[rs] * gin_half, unit_in[rs], invs[rs, :1])
        lay(narrow, rs, dx + side(narrow, 0, 4, rs).astype(F32))
    sums = nn(onehot(iota((UNIQ, size), 0) == line), side(narrow, 0, 4, every))
    acc_ref[...] = jnp.where(fresh, sums, sums + acc_ref[...])


def layer_kernel(plan, aliased, *refs):
    deltas, each = plan
    n_src = len(deltas)
    n_each = len(each)
    refs = list(refs)
    info_ref = refs.pop(0)
    msgs = [refs.pop(0) for _ in range(n_src)]
    rows_refs = [refs.pop(0) for _ in range(n_src)]
    cot_ref = refs.pop(0)
    win_ref, bin_ref, gin_ref, gmid_ref, wout_ref, bias_ref = (refs.pop(0) for _ in range(6))
    if aliased:
        refs.pop(0)
    out_ref = refs.pop(0)
    part_refs = [refs.pop(0) for _ in range(n_src)]
    loads = {}
    if not aliased:
        win_hbm, wout_hbm = win_ref, wout_ref
        win_ref, wout_ref = refs.pop(0), refs.pop(0)
    rows, ids_sc, acc, stages, blank, wsems, osems, zsems = (refs.pop(0) for _ in range(8))
    if not aliased:
        for c in ORDER:
            part = pl.ds(2 * c, 2)
            loads[c] = pltpu.make_async_copy(win_hbm.at[part], win_ref.at[part], wsems.at[c])
        loads[8] = pltpu.make_async_copy(wout_hbm, wout_ref, wsems.at[8])
    for load in loads.values():
        load.start()
    work = (win_ref, bin_ref, gin_ref, gmid_ref, wout_ref, bias_ref, *refs)
    steps = n_src * n_each

    def place_of(d):
        delta = jnp.int32(deltas[0])
        for k in range(1, n_src):
            delta = jnp.where(d == k, deltas[k], delta)
        return ((info_ref[8] - delta + 4) % 4) * 2, [info_ref[delta * 2 + b] for b in each]

    def out_copy(t, place, start, half):
        return pltpu.make_async_copy(
            stages.at[t, pl.ds(half * 128, 128)],
            out_ref.at[place, pl.ds(start, 128)],
            osems.at[t, half],
        )

    def blank_copy(d, place, k):
        return pltpu.make_async_copy(
            blank, out_ref.at[place, pl.ds(128, 128)], zsems.at[d, k]
        )

    if n_each == 2:
        blank[...] = jnp.zeros((128, D), BF)

    def step(t, carry):
        d = t // n_each
        turn = t % n_each
        base, lens = place_of(d)
        if n_each == 1:
            one = base + each[0]
            two = one
            count, count_two = lens[0], lens[0]
            long = jnp.bool_(True)
        else:
            short = (lens[0] <= 128) & (lens[1] <= 128)
            one = base + turn
            two = base + 1
            count = jnp.where(turn == 0, lens[0], lens[1])
            count_two = lens[1]
            long = jnp.logical_not(short)

        def ready(c):
            if c in loads:
                loads[c].wait()

        def work_on():
            for k in range(n_src):

                @pl.when(d == k)
                def _():
                    for b in range(n_each):
                        ids_sc[b : b + 1, :] = msgs[k][each[b] : each[b] + 1, :MAXLEN]
                    rows[...] = rows_refs[k][...]

            if n_each == 2:

                @pl.when(short)
                def _():
                    for k in range(2):
                        blank_copy(d, base + k, k).start()

            ids_one = ids_sc[pl.ds(turn, 1), :]
            ids_two = ids_sc[n_each - 1 : n_each, :]
            rows_body(
                long,
                one,
                two,
                (count, jnp.where(long, count, count_two)),
                (ids_one, ids_two),
                rows[...],
                cot_ref,
                stages.at[t],
                lambda place, start, half: out_copy(t, place, start, half).start(),
                ready,
                acc,
                turn == 0,
                work,
            )
            for k in range(n_src):

                @pl.when(d == k)
                def _():
                    part_refs[k][...] = acc[...].astype(BF)

        if n_each == 1:
            work_on()
        else:
            pl.when((turn == 0) | long)(work_on)
        return carry

    if steps == 1:
        step(jnp.int32(0), 0)
    else:
        lax.fori_loop(0, steps, step, 0)
    for d in range(n_src):
        base, lens = place_of(d)
        for half in range(2):
            out_copy(d * n_each, base, 0, half).wait()
        if n_each == 2:
            short = (lens[0] <= 128) & (lens[1] <= 128)

            @pl.when(short)
            def _():
                for k in range(2):
                    blank_copy(d, base, k).wait()

            @pl.when(jnp.logical_not(short))
            def _():
                for half in range(2):
                    out_copy(d * 2 + 1, base, 0, half).wait()


def layer(plan, info, msgs, rows, cot, weights, prior):
    deltas, each = plan
    n_src = len(deltas)
    vmem = pl.BlockSpec(memory_space=pltpu.VMEM)
    hbm = pl.BlockSpec(memory_space=pltpu.HBM)
    args = [info, *msgs, *rows, cot, *weights]
    in_specs = [pl.BlockSpec(memory_space=pltpu.SMEM)] + [vmem] * (2 * n_src + 1)
    keep = [] if prior is not None else [weights[0], weights[4]]
    spec = vmem if prior is not None else hbm
    in_specs += [spec, vmem, vmem, vmem, spec, vmem]
    alias = {}
    if prior is not None:
        alias = {len(args): 0}
        args.append(prior)
        in_specs.append(hbm)
    part = jax.ShapeDtypeStruct((UNIQ, D), BF)
    dma = pltpu.SemaphoreType.DMA
    return pl.pallas_call(
        functools.partial(layer_kernel, plan, prior is not None),
        in_specs=in_specs,
        out_specs=[hbm] + [vmem] * (n_src + len(keep)),
        scratch_shapes=[
            pltpu.VMEM((UNIQ, D), BF),
            pltpu.VMEM((8, MAXLEN), I32),
            pltpu.VMEM((UNIQ, D), F32),
            pltpu.VMEM((n_src * len(each), MAXLEN, D), BF),
            pltpu.VMEM((128, D), BF),
            dma((9,)),
            dma((n_src * len(each), 2)),
            dma((n_src, 2)),
            pltpu.VMEM((16, MAXLEN, 128), BF),
            pltpu.VMEM((16, MAXLEN, 128), BF),
            pltpu.VMEM((HEADS, 2, MAXLEN, 128), BF),
            pltpu.VMEM((HEADS, 2, MAXLEN, 128), BF),
            pltpu.VMEM((16, MAXLEN, 128), BF),
            pltpu.VMEM((MAXLEN, D), F32),
            pltpu.VMEM((MAXLEN, D), F32),
            pltpu.VMEM((MAXLEN, D), F32),
            pltpu.VMEM((MAXLEN, 128), F32),
            pltpu.VMEM((4, MAXLEN, 128), BF),
            pltpu.VMEM((MAXLEN, D), F32),
        ],
        out_shape=[jax.ShapeDtypeStruct(cot.shape, BF)]
        + [part] * n_src
        + [jax.ShapeDtypeStruct(w.shape, BF) for w in keep],
        input_output_aliases=alias,
        compiler_params=params(),
        name="layer",
    )(*args)


def info_kernel(seq_ref, *refs):
    out_ref = refs[-1]
    for d in range(4):
        for b in range(2):
            out_ref[2 * d + b] = refs[d][b, MAXLEN]
    out_ref[8] = seq_ref[0]


def scalars(seq, msgs):
    smem = pl.BlockSpec(memory_space=pltpu.SMEM)
    return pl.pallas_call(
        info_kernel,
        in_specs=[smem] * 5,
        out_specs=smem,
        out_shape=jax.ShapeDtypeStruct((16,), I32),
        compiler_params=params(),
        name="scalars",
    )(seq, *msgs)


def expand_kernel(pos_ref, *refs):
    out_ref = refs[-1]
    total = refs[0][...].astype(F32)
    for r in refs[1:-1]:
        total = total + r[...].astype(F32)
    total = total.astype(BF)
    row = iota((8 * DEVICES, UNIQ), 0)
    pos = pos_ref[...]
    upper = nn(onehot(row == pos), total[:, : D // 2])
    lower = nn(onehot(row == pos + 4), total[:, D // 2 :])
    out_ref[...] = (upper + lower).astype(BF)


def expand(pos, parts):
    return pl.pallas_call(
        expand_kernel,
        out_shape=jax.ShapeDtypeStruct((8 * DEVICES, D // 2), BF),
        compiler_params=params(),
        name="expand",
    )(pos, *parts)


def asked_line_kernel(asked_ref, out_ref):
    parts = []
    shape = (DEVICES, 4 * DEVICES)
    spread = onehot(iota(shape, 0) == (iota(shape, 1) >> 2))
    for part in asked_parts(asked_ref):
        square = jnp.concatenate([part.astype(F32), jnp.zeros((DEVICES, 124), F32)], axis=1)
        parts.append(nn(square.T[:8].astype(BF), spread))
    value = parts[0] * 32.0 + parts[1]
    mine = iota((8, 4 * DEVICES), 0) == (iota((8, 4 * DEVICES), 1) & 3)
    out_ref[...] = jnp.sum(jnp.where(mine, value, 0.0), axis=0, keepdims=True).astype(I32)


def asked_line(asked):
    return pl.pallas_call(
        asked_line_kernel,
        out_shape=jax.ShapeDtypeStruct((1, 4 * DEVICES), I32),
        compiler_params=params(),
        name="asked_line",
    )(asked)


def scatter_kernel(line_ref, landed_ref, out_ref, whole_ref):
    size = out_ref.shape[0]

    @pl.when(pl.program_id(0) == 0)
    def _():
        whole_ref[...] = from_halves(landed_ref[...].astype(F32)).astype(BF)

    row = iota((size, 4 * DEVICES), 0) + pl.program_id(0) * size
    out_ref[...] = nn(onehot(row == line_ref[...]), whole_ref[...])


def scatter(line, landed):
    size = 256
    whole = lambda a: pl.BlockSpec(a.shape, lambda i: (0, 0), pipeline_mode=pl.Buffered(1))
    return pl.pallas_call(
        scatter_kernel,
        grid=(ROWS_DEV // size,),
        in_specs=[whole(line), whole(landed)],
        out_specs=pl.BlockSpec((size, D), lambda i: (i, 0)),
        out_shape=jax.ShapeDtypeStruct((ROWS_DEV, D), F32),
        scratch_shapes=[pltpu.VMEM((4 * DEVICES, D), BF)],
        compiler_params=params(dimension_semantics=("arbitrary",)),
        name="scatter",
    )(line, landed)


def ring(delta):
    return [(i, (i + delta) % 4) for i in range(4)]


def exchange(x, shape):
    got = lax.all_to_all(x.reshape(shape), ("emb", "seq"), split_axis=0, concat_axis=0, tiled=True)
    return got.reshape(x.shape)


PLANS = (((0,), (0,)), ((1,), (0, 1)), ((3, 2), (0, 1)), ((0,), (1,)))


def program(
    item_table,
    unique_ids,
    inverse,
    lengths,
    assignment,
    proj_in,
    bias_in,
    gain_in,
    gain_mid,
    proj_out,
    position_bias,
    cotangent,
):
    seq = lax.axis_index("seq").astype(I32).reshape(1)
    req, pos, *sent = pack(assignment, lengths, seq, unique_ids, inverse)
    asked = exchange(req, (DEVICES, 1, 4))
    msgs = [sent[0]] + [lax.ppermute(sent[d], "seq", ring(d)) for d in (1, 2, 3)]
    bias, pos_rows, win, wout = tables(position_bias, pos, proj_in, proj_out)
    answer = answer_rows(asked, item_table)
    got = exchange(answer, (DEVICES, 8, D // 2))
    info = scalars(seq, msgs)
    got, info = lax.optimization_barrier((got, info))
    line = asked_line(asked)
    own = compact(pos_rows, got)
    rows = [own]
    for d in (1, 2, 3):
        rows.append(lax.ppermute(own, "seq", ring(d)))
    weights = (
        in_hbm(win),
        bias_in.reshape(1, 4 * D),
        gain_in.reshape(1, D),
        gain_mid.reshape(1, D),
        in_hbm(wout),
        bias,
    )
    outputs = None
    sums = []
    for plan in PLANS:
        outputs, *parts = layer(
            plan,
            info,
            [msgs[d] for d in plan[0]],
            [rows[d] for d in plan[0]],
            cotangent,
            weights,
            outputs,
        )
        if len(parts) > len(plan[0]):
            weights = (parts[-2], *weights[1:4], parts[-1], weights[5])
        for d, part in zip(plan[0], parts):
            sums.append(part if d == 0 else lax.ppermute(part, "seq", ring(-d)))
    landed = exchange(expand(pos, sums), (DEVICES, 8, D // 2))
    return (outputs, scatter(line, landed))


def solution(mesh):
    both = ("emb", "seq")
    in_specs = (
        P(both, None),
        P(both),
        P(both, None),
        P(both),
        P(both),
        P(),
        P(),
        P(),
        P(),
        P(),
        P(),
        P(both, None, None),
    )
    out_specs = (P(both, None, None), P(both, None))
    return jax.shard_map(program, mesh=mesh, in_specs=in_specs, out_specs=out_specs, check_vma=False)
```

```python
import functools

import jax
import jax.numpy as jnp
from jax import lax
from jax.experimental import pallas as pl
from jax.experimental.pallas import tpu as pltpu
from jax.sharding import PartitionSpec as P

D = 512
HEADS = 4
HEAD = 128
MAXLEN = 256
UNIQ = 256
ROWS_DEV = 1024
DEVICES = 128
SCALE = HEAD**-0.5
EPS = 1e-05
MASKED = -1e30
BF = jnp.bfloat16
F32 = jnp.float32
I32 = jnp.int32


def nn(a, b):
    return lax.dot_general(a, b, (((1,), (0,)), ((), ())), preferred_element_type=F32)


def nt(a, b):
    return lax.dot_general(a, b, (((1,), (1,)), ((), ())), preferred_element_type=F32)


def tn(a, b):
    return lax.dot_general(a, b, (((0,), (0,)), ((), ())), preferred_element_type=F32)


def iota(shape, dim):
    return lax.broadcasted_iota(I32, shape, dim)


def onehot(mask):
    return jnp.where(mask, 1.0, 0.0).astype(BF)


def in_hbm(x):
    return pltpu.with_memory_space_constraint(x, pltpu.HBM)


def params(**kw):
    return pltpu.CompilerParams(vmem_limit_bytes=24 << 20, **kw)


def pack_kernel(assign_hbm, len_hbm, seq_ref, ids_hbm, inv_hbm, req_ref, pos_ref, *refs):
    msg_refs = refs[:4]
    assign_ref, len_ref, ids_ref, inv_ref, sems = refs[4:]
    loads = [
        pltpu.make_async_copy(src, dst, sems.at[k])
        for k, (src, dst) in enumerate(
            (
                (ids_hbm, ids_ref),
                (inv_hbm, inv_ref),
                (assign_hbm, assign_ref),
                (len_hbm, len_ref),
            )
        )
    ]
    for load in loads:
        load.start()
    loads[0].wait()
    ids = ids_ref[...]
    owner = ids >> 10
    local = (ids & (ROWS_DEV - 1)).astype(F32)
    held = iota((DEVICES, UNIQ), 0) == owner
    earlier = onehot(iota((UNIQ, UNIQ), 0) < iota((UNIQ, UNIQ), 1))
    before = nn(onehot(held), earlier)
    rank = jnp.sum(jnp.where(held, before, 0.0), axis=0, keepdims=True)
    pos_ref[...] = owner * 8 + rank.astype(I32)
    lane = iota((DEVICES, 4), 1)
    req = jnp.zeros((DEVICES, 4), F32)
    for r in range(4):
        chosen = held & (before == float(r))
        col = jnp.sum(jnp.where(chosen, ROWS_DEV - local, 0.0), axis=1, keepdims=True)
        req = jnp.where(lane == r, ROWS_DEV - col, req)
    req_ref[...] = req.astype(I32)
    for load in loads[1:]:
        load.wait()
    seq = seq_ref[0]
    for j in range(8):
        place = assign_ref[j]
        delta = (place // 8 - seq + 4) % 4
        half = place % 2
        row = jnp.concatenate(
            [inv_ref[j : j + 1, :], jnp.full((1, 128), len_ref[j], I32)], axis=1
        )
        for d in range(4):
            for b in range(2):

                @pl.when((delta == d) & (half == b))
                def _():
                    msg_refs[d][b : b + 1, :] = row


def pack(assignment, lengths, seq, ids, inverse):
    smem = pl.BlockSpec(memory_space=pltpu.SMEM)
    vmem = pl.BlockSpec(memory_space=pltpu.VMEM)
    hbm = pl.BlockSpec(memory_space=pltpu.HBM)
    return pl.pallas_call(
        pack_kernel,
        in_specs=[hbm, hbm, smem, hbm, hbm],
        scratch_shapes=[
            pltpu.SMEM((8,), I32),
            pltpu.SMEM((8,), I32),
            pltpu.VMEM((1, UNIQ), I32),
            pltpu.VMEM((8, MAXLEN), I32),
            pltpu.SemaphoreType.DMA((4,)),
        ],
        out_specs=[vmem] * 6,
        out_shape=[
            jax.ShapeDtypeStruct((DEVICES, 4), I32),
            jax.ShapeDtypeStruct((1, UNIQ), I32),
        ]
        + [jax.ShapeDtypeStruct((2, MAXLEN + 128), I32)] * 4,
        compiler_params=params(),
        name="pack",
    )(in_hbm(assignment), in_hbm(lengths), seq, in_hbm(ids.reshape(1, UNIQ)), in_hbm(inverse))


def tables_kernel(flipped_ref, pos_ref, win_hbm, wout_hbm, *refs):
    bias_ref, pos_rows_ref, winb_hbm, woutb_hbm, win_ref, wout_ref, winb_ref, woutb_ref, sems = refs
    loads = [
        pltpu.make_async_copy(win_hbm, win_ref, sems.at[0]),
        pltpu.make_async_copy(wout_hbm, wout_ref, sems.at[1]),
    ]
    stores = [
        pltpu.make_async_copy(winb_ref, winb_hbm, sems.at[2]),
        pltpu.make_async_copy(woutb_ref, woutb_hbm, sems.at[3]),
    ]
    for load in loads:
        load.start()
    i = iota((MAXLEN, MAXLEN), 0)
    j = iota((MAXLEN, MAXLEN), 1)
    for h in range(HEADS):
        line = jnp.broadcast_to(flipped_ref[h : h + 1, :], (MAXLEN, MAXLEN))
        spread = pltpu.roll(line, 1, 1, stride=1, stride_axis=0)
        full = jnp.where(j <= i, 0.5 * spread, MASKED)
        bias_ref[h] = full[:, :128]
    pos = jnp.broadcast_to(pos_ref[...], (UNIQ, UNIQ)).astype(F32)
    col = jnp.sum(jnp.where(i == j, pos, 0.0), axis=1, keepdims=True)
    pos_rows_ref[...] = jnp.broadcast_to(col.astype(I32), (UNIQ, 128))
    for load, store, src, dst in zip(loads, stores, (win_ref, wout_ref), (winb_ref, woutb_ref)):
        load.wait()
        for c in range(dst.shape[0]):
            dst[c] = src[:, pl.ds(c * 128, 128)]
        store.start()
    for store in stores:
        store.wait()


def tables(position_bias, pos, proj_in, proj_out):
    vmem = pl.BlockSpec(memory_space=pltpu.VMEM)
    hbm = pl.BlockSpec(memory_space=pltpu.HBM)
    return pl.pallas_call(
        tables_kernel,
        out_shape=[
            jax.ShapeDtypeStruct((HEADS, MAXLEN, 128), F32),
            jax.ShapeDtypeStruct((UNIQ, 128), I32),
            pltpu.HBM((16, D, 128), BF),
            pltpu.HBM((4, D, 128), BF),
        ],
        in_specs=[vmem, vmem, hbm, hbm],
        out_specs=[vmem, vmem, hbm, hbm],
        scratch_shapes=[
            pltpu.VMEM((D, 4 * D), BF),
            pltpu.VMEM((D, D), BF),
            pltpu.VMEM((16, D, 128), BF),
            pltpu.VMEM((4, D, 128), BF),
            pltpu.SemaphoreType.DMA((4,)),
        ],
        compiler_params=params(),
        name="tables",
    )(position_bias[:, ::-1], pos, in_hbm(proj_in), in_hbm(proj_out))


def asked_parts(asked_ref):
    asked = asked_ref[...]
    return (asked >> 5).astype(BF), (asked & 31).astype(BF)


def to_halves(x):
    groups = x.shape[0] // 8
    upper = iota((groups, 8, D // 2), 1) < 4
    low = x[:, : D // 2].reshape(groups, 8, D // 2)
    high = x[:, D // 2 :].reshape(groups, 8, D // 2)
    even = jnp.where(upper, low, pltpu.roll(high, 4, 1))
    odd = jnp.where(upper, pltpu.roll(low, 4, 1), high)
    both = jnp.concatenate([even[:, None], odd[:, None]], axis=1)
    return both.reshape(groups * 16, D // 2)


def from_halves(x):
    groups = x.shape[0] // 16
    upper = iota((groups, 8, D // 2), 1) < 4
    pairs = x.reshape(groups, 2, 8, D // 2)
    even = pairs[:, 0]
    odd = pairs[:, 1]
    low = jnp.where(upper, even, pltpu.roll(odd, 4, 1))
    high = jnp.where(upper, pltpu.roll(even, 4, 1), odd)
    flat = (groups * 8, D // 2)
    return jnp.concatenate([low.reshape(flat), high.reshape(flat)], axis=1)


def answer_kernel(asked_ref, table_hbm, out_ref, table_ref, pick_ref, sem):
    loads = []
    for c in range(4):
        part = pl.ds(c * 256, 256)
        loads.append(pltpu.make_async_copy(table_hbm.at[part], table_ref.at[part], sem.at[c]))
    for load in loads:
        load.start()
    high, low = asked_parts(asked_ref)
    count = 4 * DEVICES
    spread = onehot((iota((count, DEVICES), 0) >> 2) == iota((count, DEVICES), 1))
    value = nn(spread, high) * 32.0 + nn(spread, low)
    mine = iota((count, 4), 1) == (iota((count, 4), 0) & 3)
    col = jnp.sum(jnp.where(mine, value, 0.0), axis=1, keepdims=True).astype(I32)
    pick_ref[...] = onehot(iota((count, ROWS_DEV), 1) == col)
    for load in loads:
        load.wait()
    for c in range(2):
        rows = nn(pick_ref[pl.ds(c * 256, 256), :], table_ref[...])
        out_ref[pl.ds(c * 512, 512), :] = to_halves(rows).astype(BF)


def answer_rows(asked, table):
    return pl.pallas_call(
        answer_kernel,
        in_specs=[pl.BlockSpec(memory_space=pltpu.VMEM), pl.BlockSpec(memory_space=pltpu.HBM)],
        out_shape=jax.ShapeDtypeStruct((8 * DEVICES, D // 2), BF),
        scratch_shapes=[
            pltpu.VMEM((ROWS_DEV, D), BF),
            pltpu.VMEM((4 * DEVICES, ROWS_DEV), BF),
            pltpu.SemaphoreType.DMA((4,)),
        ],
        compiler_params=params(),
        name="answer",
    )(asked, in_hbm(table))


def compact_kernel(pos_ref, got_ref, out_ref):
    pos = pos_ref[:, :1]
    lane = iota((UNIQ, 8 * DEVICES), 1)
    for half in range(2):
        pick = onehot(lane == pos + 4 * half)
        out_ref[:, pl.ds(half * 256, 256)] = nn(pick, got_ref[...]).astype(BF)


def compact(pos_rows, got):
    return pl.pallas_call(
        compact_kernel,
        out_shape=jax.ShapeDtypeStruct((UNIQ, D), BF),
        compiler_params=params(),
        name="compact",
    )(pos_rows, got)


def row_mean(x):
    return jnp.sum(x, axis=-1, keepdims=True) * (1.0 / D)


def norm_parts(x):
    center = x - row_mean(x)
    spread = row_mean(center * center)
    inv = lax.rsqrt(spread + EPS)
    return center * inv, inv


def norm_grad(g, unit, inv):
    return inv * (g - row_mean(g) - unit * row_mean(g * unit))


def chunks(size, step=64):
    return [slice(r, r + step) for r in range(0, size, step)]


def side(ref, first, count, rs=slice(None)):
    return jnp.concatenate([ref[c, rs] for c in range(first, first + count)], axis=1)


def lay(ref, rs, value):
    for c in range(value.shape[1] // 128):
        ref[c, rs] = value[:, c * 128 : (c + 1) * 128].astype(BF)


ORDER = (6, 7, 4, 5, 2, 3, 0, 1)


def rows_body(long, one, two, counts, msg, rows, cot_ref, stage_ref, send, ready, acc_ref, fresh, refs):
    (win_ref, bin_ref, gin_ref, gmid_ref, wout_ref, bias_ref) = refs[:6]
    (hid, slope, wts, wslope, dpre, xs, unit_in, unit_mid, invs, narrow, wide) = refs[6:]
    size = MAXLEN
    every = slice(0, size)
    firsts, seconds = slice(0, 128), slice(128, 256)
    gin_half = 0.5 * gin_ref[...]
    start = jnp.where(long, 128, 0)
    lane = iota((1, 128), 1)
    ids_one, ids_two = msg
    line = jnp.concatenate(
        [
            jnp.where(lane < counts[0], ids_one[:, :128], -1),
            jnp.where(lane + start < counts[1], jnp.where(long, ids_one[:, 128:], ids_two[:, :128]), -1),
        ],
        axis=1,
    )
    cols = jnp.broadcast_to(line, (8, size)).astype(F32).T[:, :1].astype(I32)
    xs[...] = nn(onehot(iota((size, UNIQ), 1) == cols), rows)
    for rs in chunks(size):
        unit, inv = norm_parts(xs[rs])
        unit_in[rs] = unit
        invs[rs] = jnp.broadcast_to(inv, (rs.stop - rs.start, 128))
        lay(narrow, rs, unit * gin_half)
    for c in ORDER:
        ready(c)
        pre = nn(side(narrow, 0, 4, every), side(win_ref, 2 * c, 2))
        for k in range(2):
            blk = 2 * c + k
            half = pre[:, k * 128 : (k + 1) * 128] + 0.5 * bin_ref[:, pl.ds(blk * 128, 128)]
            up = 1.0 + jnp.tanh(half)
            act = (half * up).astype(BF)
            up = up.astype(BF)
            hid[blk] = act
            slope[blk] = up + act * (jnp.array(2.0, BF) - up)
    valid = [iota((128, 1), 0) < counts[0], iota((128, 1), 0) + start < counts[1]]
    per = []
    for part in range(2):
        inverse = 1.0 / jnp.full((1, 1), jnp.maximum(counts[part], 1), I32).astype(F32)
        per.append(jnp.where(valid[part], inverse, 0.0))
    cross = per[1] * jnp.where(long, 1.0, 0.0)
    blocks = ((0, 0, per[0]), (1, 1, per[1]), (1, 0, cross))
    cut = lambda i: slice(i * 128, i * 128 + 128)
    for h in range(HEADS):
        for bi, bj, scale in blocks:
            bias = bias_ref[h, (bi - bj) * 128 : (bi - bj) * 128 + 128, :]
            half = nt(hid[8 + h, cut(bi)], hid[12 + h, cut(bj)]) * (0.5 * SCALE) + bias
            up = 1.0 + jnp.tanh(half)
            act = half * up
            wts[h, bj, cut(bi)] = (act * scale).astype(BF)
            wslope[h, bj, cut(bi)] = ((up + act * (2.0 - up)) * (scale * (0.5 * SCALE))).astype(BF)
    for h in range(HEADS):
        for bi in range(2):
            wide[cut(bi), pl.ds(h * HEAD, HEAD)] = nn(
                side(wts.at[h], 0, bi + 1, cut(bi)), hid[4 + h, : (bi + 1) * 128]
            )
    for rs in chunks(size):
        unit, inv = norm_parts(wide[rs])
        unit_mid[rs] = unit
        lay(narrow, rs, unit * gmid_ref[...] * side(hid, 0, 4, rs).astype(F32))
        wide[rs, :128] = jnp.broadcast_to(inv, (rs.stop - rs.start, 128))
    ready(8)
    result = nn(side(narrow, 0, 4, every), side(wout_ref, 0, 4))
    other = jnp.where(long, one, two)
    for half, rs in enumerate((firsts, seconds)):
        stage_ref[rs] = jnp.where(valid[half], xs[rs] + result[rs], 0.0).astype(BF)
    send(one, 0, 0)
    send(other, pl.multiple_of(start, 128), 1)
    zero = jnp.zeros((), BF)
    lay(narrow, firsts, jnp.where(valid[0], cot_ref[one, :128, :], zero))
    lay(
        narrow,
        seconds,
        jnp.where(valid[1], cot_ref[other, pl.ds(pl.multiple_of(start, 128), 128), :], zero),
    )
    xs[...] = nt(side(narrow, 0, 4, every), side(wout_ref, 0, 4))
    for rs in chunks(size):
        unit = unit_mid[rs]
        inv = wide[rs, :1]
        grown = xs[rs] * gmid_ref[...]
        scaled = grown * unit
        for c in range(4):
            dpre[c, rs] = scaled[:, c * 128 : (c + 1) * 128].astype(BF) * slope[c, rs]
        lay(hid, rs, norm_grad(grown * side(hid, 0, 4, rs).astype(F32), unit, inv))
    for h in range(HEADS):
        for bi, bj, scale in blocks:
            ds = nt(hid[h, cut(bi)], hid[4 + h, cut(bj)]).astype(BF)
            wslope[h, bj, cut(bi)] = ds * wslope[h, bj, cut(bi)]
    for h in range(HEADS):
        for bi in range(2):
            dq = nn(side(wslope.at[h], 0, bi + 1, cut(bi)), hid[12 + h, : (bi + 1) * 128])
            dpre[8 + h, cut(bi)] = dq.astype(BF) * slope[8 + h, cut(bi)]
    for h in range(HEADS):
        for bj in range(2):
            qs = slice(bj * 128, size)
            dv = tn(wts[h, bj, qs], hid[h, qs])
            dpre[4 + h, cut(bj)] = dv.astype(BF) * slope[4 + h, cut(bj)]
            dk = tn(wslope[h, bj, qs], hid[8 + h, qs])
            dpre[12 + h, cut(bj)] = dk.astype(BF) * slope[12 + h, cut(bj)]
    wide[...] = nt(side(dpre, 0, 16, every), side(win_ref, 0, 16))
    for rs in chunks(size):
        dx = norm_grad(wide[rs] * gin_half, unit_in[rs], invs[rs, :1])
        lay(narrow, rs, dx + side(narrow, 0, 4, rs).astype(F32))
    sums = nn(onehot(iota((UNIQ, size), 0) == line), side(narrow, 0, 4, every))
    acc_ref[...] = jnp.where(fresh, sums, sums + acc_ref[...])


BOTH, EARLY, LATE = range(3)


def layer_kernel(plan, aliased, *refs):
    deltas, mode = plan
    n_src = len(deltas)
    refs = list(refs)
    info_ref = refs.pop(0)
    msgs = [refs.pop(0) for _ in range(n_src)]
    rows_refs = [refs.pop(0) for _ in range(n_src)]
    cot_ref = refs.pop(0)
    win_ref, bin_ref, gin_ref, gmid_ref, wout_ref, bias_ref = (refs.pop(0) for _ in range(6))
    if aliased:
        refs.pop(0)
    out_ref = refs.pop(0)
    part_refs = [refs.pop(0) for _ in range(n_src)]
    win_hbm, wout_hbm = win_ref, wout_ref
    if not aliased:
        win_ref, wout_ref = refs.pop(0), refs.pop(0)
    rows, ids_sc, acc, stages, blank, wsems, osems, zsems = (refs.pop(0) for _ in range(8))
    loads = {}
    if not aliased:
        for c in ORDER:
            part = pl.ds(2 * c, 2)
            loads[c] = pltpu.make_async_copy(win_hbm.at[part], win_ref.at[part], wsems.at[c])
        loads[8] = pltpu.make_async_copy(wout_hbm, wout_ref, wsems.at[8])
    for load in loads.values():
        load.start()
    work = (win_ref, bin_ref, gin_ref, gmid_ref, wout_ref, bias_ref, *refs)

    def ready(c):
        if c in loads:
            loads[c].wait()

    turns = 2 if mode == BOTH else 1
    steps = n_src * turns
    blank[...] = jnp.zeros((128, D), BF)

    def source(d):
        delta = jnp.int32(deltas[0])
        for k in range(1, n_src):
            delta = jnp.where(d == k, deltas[k], delta)
        lens = [info_ref[delta * 2 + b] for b in range(2)]
        base = ((info_ref[8] - delta + 4) % 4) * 2
        return base, lens, (lens[0] <= 128) & (lens[1] <= 128)

    def out_copy(t, place, start, half):
        return pltpu.make_async_copy(
            stages.at[t, pl.ds(half * 128, 128)],
            out_ref.at[place, pl.ds(start, 128)],
            osems.at[t, half],
        )

    def blank_copy(d, place, k):
        return pltpu.make_async_copy(
            blank, out_ref.at[place, pl.ds(128, 128)], zsems.at[d, k]
        )

    def step(t, carry):
        d = t // turns
        base, lens, short = source(d)
        long = jnp.logical_not(short)
        if mode == BOTH:
            turn = t % turns
            go = (turn == 0) | long
        elif mode == EARLY:
            turn = jnp.int32(0)
            go = long
        else:
            turn = jnp.where(short, 0, 1)
            go = None
        count = jnp.where(turn == 0, lens[0], lens[1])

        def work_on():
            for k in range(n_src):

                @pl.when(d == k)
                def _():
                    ids_sc[:2, :] = msgs[k][:, :MAXLEN]
                    rows[...] = rows_refs[k][...]

            if mode != EARLY:

                @pl.when(short)
                def _():
                    for k in range(2):
                        blank_copy(d, base + k, k).start()

            rows_body(
                long,
                base + turn,
                base + 1,
                (count, jnp.where(long, count, lens[1])),
                (ids_sc[pl.ds(turn, 1), :], ids_sc[1:2, :]),
                rows[...],
                cot_ref,
                stages.at[t],
                lambda place, start, half: out_copy(t, place, start, half).start(),
                ready,
                acc,
                (turn == 0) | (mode == LATE),
                work,
            )
            for k in range(n_src):

                @pl.when(d == k)
                def _():
                    part_refs[k][...] = acc[...].astype(BF)

        if mode == EARLY:

            @pl.when(short)
            def _():
                part_refs[0][...] = jnp.zeros((UNIQ, D), BF)
                for load in loads.values():
                    load.wait()

        if go is None:
            work_on()
        else:
            pl.when(go)(work_on)
        return carry

    if steps == 1:
        step(jnp.int32(0), 0)
    else:
        lax.fori_loop(0, steps, step, 0)
    for d in range(n_src):
        base, _, short = source(d)

        def sent(t):
            for half in range(2):
                out_copy(t, base, 0, half).wait()

        if mode == EARLY:
            pl.when(jnp.logical_not(short))(functools.partial(sent, 0))
        else:
            sent(d * turns)

            @pl.when(short)
            def _():
                for k in range(2):
                    blank_copy(d, base, k).wait()

            if mode == BOTH:
                pl.when(jnp.logical_not(short))(functools.partial(sent, d * turns + 1))


def layer(plan, info, msgs, rows, cot, weights, prior):
    deltas, mode = plan
    n_src = len(deltas)
    steps = n_src * (2 if mode == BOTH else 1)
    vmem = pl.BlockSpec(memory_space=pltpu.VMEM)
    hbm = pl.BlockSpec(memory_space=pltpu.HBM)
    args = [info, *msgs, *rows, cot, *weights]
    keep = [] if prior is not None else [weights[0], weights[4]]
    spec = vmem if prior is not None else hbm
    in_specs = [pl.BlockSpec(memory_space=pltpu.SMEM)] + [vmem] * (2 * n_src + 1)
    in_specs += [spec, vmem, vmem, vmem, spec, vmem]
    alias = {}
    if prior is not None:
        alias = {len(args): 0}
        args.append(prior)
        in_specs.append(hbm)
    part = jax.ShapeDtypeStruct((UNIQ, D), BF)
    dma = pltpu.SemaphoreType.DMA
    return pl.pallas_call(
        functools.partial(layer_kernel, plan, prior is not None),
        in_specs=in_specs,
        out_specs=[hbm] + [vmem] * (n_src + len(keep)),
        scratch_shapes=[
            pltpu.VMEM((UNIQ, D), BF),
            pltpu.VMEM((8, MAXLEN), I32),
            pltpu.VMEM((UNIQ, D), F32),
            pltpu.VMEM((steps, MAXLEN, D), BF),
            pltpu.VMEM((128, D), BF),
            dma((9,)),
            dma((steps, 2)),
            dma((n_src, 2)),
            pltpu.VMEM((16, MAXLEN, 128), BF),
            pltpu.VMEM((16, MAXLEN, 128), BF),
            pltpu.VMEM((HEADS, 2, MAXLEN, 128), BF),
            pltpu.VMEM((HEADS, 2, MAXLEN, 128), BF),
            pltpu.VMEM((16, MAXLEN, 128), BF),
            pltpu.VMEM((MAXLEN, D), F32),
            pltpu.VMEM((MAXLEN, D), F32),
            pltpu.VMEM((MAXLEN, D), F32),
            pltpu.VMEM((MAXLEN, 128), F32),
            pltpu.VMEM((4, MAXLEN, 128), BF),
            pltpu.VMEM((MAXLEN, D), F32),
        ],
        out_shape=[jax.ShapeDtypeStruct(cot.shape, BF)]
        + [part] * n_src
        + [jax.ShapeDtypeStruct(w.shape, BF) for w in keep],
        input_output_aliases=alias,
        compiler_params=params(),
        name="layer",
    )(*args)


def info_kernel(seq_ref, *refs):
    out_ref = refs[-1]
    for d in range(4):
        for b in range(2):
            out_ref[2 * d + b] = refs[d][b, MAXLEN]
    out_ref[8] = seq_ref[0]


def scalars(seq, msgs):
    smem = pl.BlockSpec(memory_space=pltpu.SMEM)
    return pl.pallas_call(
        info_kernel,
        in_specs=[smem] * 5,
        out_specs=smem,
        out_shape=jax.ShapeDtypeStruct((16,), I32),
        compiler_params=params(),
        name="scalars",
    )(seq, *msgs)


def expand_kernel(pos_ref, *refs):
    out_ref = refs[-1]
    total = refs[0][...].astype(F32)
    for r in refs[1:-1]:
        total = total + r[...].astype(F32)
    total = total.astype(BF)
    row = iota((8 * DEVICES, UNIQ), 0)
    pos = pos_ref[...]
    upper = nn(onehot(row == pos), total[:, : D // 2])
    lower = nn(onehot(row == pos + 4), total[:, D // 2 :])
    out_ref[...] = (upper + lower).astype(BF)


def expand(pos, parts):
    return pl.pallas_call(
        expand_kernel,
        out_shape=jax.ShapeDtypeStruct((8 * DEVICES, D // 2), BF),
        compiler_params=params(),
        name="expand",
    )(pos, *parts)


def asked_line_kernel(asked_ref, out_ref):
    parts = []
    shape = (DEVICES, 4 * DEVICES)
    spread = onehot(iota(shape, 0) == (iota(shape, 1) >> 2))
    for part in asked_parts(asked_ref):
        square = jnp.concatenate([part.astype(F32), jnp.zeros((DEVICES, 124), F32)], axis=1)
        parts.append(nn(square.T[:8].astype(BF), spread))
    value = parts[0] * 32.0 + parts[1]
    mine = iota((8, 4 * DEVICES), 0) == (iota((8, 4 * DEVICES), 1) & 3)
    out_ref[...] = jnp.sum(jnp.where(mine, value, 0.0), axis=0, keepdims=True).astype(I32)


def asked_line(asked):
    return pl.pallas_call(
        asked_line_kernel,
        out_shape=jax.ShapeDtypeStruct((1, 4 * DEVICES), I32),
        compiler_params=params(),
        name="asked_line",
    )(asked)


def scatter_kernel(line_ref, landed_ref, out_hbm, whole_ref, rows_ref, sems):
    whole_ref[...] = from_halves(landed_ref[...].astype(F32)).astype(BF)
    size = 256
    moves = []
    for c in range(ROWS_DEV // size):
        row = iota((size, 4 * DEVICES), 0) + c * size
        rows_ref[pl.ds(c * size, size), :] = nn(onehot(row == line_ref[...]), whole_ref[...])
        for k in range(2):
            part = pl.ds(c * size + k * 128, 128)
            move = pltpu.make_async_copy(rows_ref.at[part], out_hbm.at[part], sems.at[2 * c + k])
            move.start()
            moves.append(move)
    for move in moves:
        move.wait()


def scatter(line, landed):
    vmem = pl.BlockSpec(memory_space=pltpu.VMEM)
    return pl.pallas_call(
        scatter_kernel,
        in_specs=[vmem, vmem],
        out_specs=pl.BlockSpec(memory_space=pltpu.HBM),
        out_shape=jax.ShapeDtypeStruct((ROWS_DEV, D), F32),
        scratch_shapes=[
            pltpu.VMEM((4 * DEVICES, D), BF),
            pltpu.VMEM((ROWS_DEV, D), F32),
            pltpu.SemaphoreType.DMA((8,)),
        ],
        compiler_params=params(),
        name="scatter",
    )(line, landed)


def ring(delta):
    return [(i, (i + delta) % 4) for i in range(4)]


def exchange(x, shape):
    got = lax.all_to_all(x.reshape(shape), ("emb", "seq"), split_axis=0, concat_axis=0, tiled=True)
    return got.reshape(x.shape)


PLANS = (((0,), EARLY), ((1,), BOTH), ((3, 2), BOTH), ((0,), LATE))


def program(
    item_table,
    unique_ids,
    inverse,
    lengths,
    assignment,
    proj_in,
    bias_in,
    gain_in,
    gain_mid,
    proj_out,
    position_bias,
    cotangent,
):
    seq = lax.axis_index("seq").astype(I32).reshape(1)
    req, pos, *sent = pack(assignment, lengths, seq, unique_ids, inverse)
    asked = exchange(req, (DEVICES, 1, 4))
    msgs = [sent[0]] + [lax.ppermute(sent[d], "seq", ring(d)) for d in (1, 2, 3)]
    bias, pos_rows, win, wout = tables(position_bias, pos, proj_in, proj_out)
    answer = answer_rows(asked, item_table)
    got = exchange(answer, (DEVICES, 8, D // 2))
    info = scalars(seq, msgs)
    got, info = lax.optimization_barrier((got, info))
    line = asked_line(asked)
    own = compact(pos_rows, got)
    rows = [own]
    for d in (1, 2, 3):
        rows.append(lax.ppermute(own, "seq", ring(d)))
    weights = (
        in_hbm(win),
        bias_in.reshape(1, 4 * D),
        gain_in.reshape(1, D),
        gain_mid.reshape(1, D),
        in_hbm(wout),
        bias,
    )
    outputs = None
    sums = []
    for plan in PLANS:
        outputs, *parts = layer(
            plan,
            info,
            [msgs[d] for d in plan[0]],
            [rows[d] for d in plan[0]],
            cotangent,
            weights,
            outputs,
        )
        if len(parts) > len(plan[0]):
            weights = (parts[-2], *weights[1:4], parts[-1], weights[5])
        for d, part in zip(plan[0], parts):
            sums.append(part if d == 0 else lax.ppermute(part, "seq", ring(-d)))
    landed = exchange(expand(pos, sums), (DEVICES, 8, D // 2))
    return (outputs, scatter(line, landed))


def solution(mesh):
    both = ("emb", "seq")
    in_specs = (
        P(both, None),
        P(both),
        P(both, None),
        P(both),
        P(both),
        P(),
        P(),
        P(),
        P(),
        P(),
        P(),
        P(both, None, None),
    )
    out_specs = (P(both, None, None), P(both, None))
    return jax.shard_map(program, mesh=mesh, in_specs=in_specs, out_specs=out_specs, check_vma=False)
```

```python
import functools

import jax
import jax.numpy as jnp
from jax import lax
from jax.experimental import pallas as pl
from jax.experimental.pallas import tpu as pltpu
from jax.sharding import PartitionSpec as P

D = 512
HEADS = 4
HEAD = 128
MAXLEN = 256
UNIQ = 256
ROWS_DEV = 1024
DEVICES = 128
SCALE = HEAD**-0.5
EPS = 1e-05
MASKED = -1e30
BF = jnp.bfloat16
F32 = jnp.float32
I32 = jnp.int32


def nn(a, b):
    return lax.dot_general(a, b, (((1,), (0,)), ((), ())), preferred_element_type=F32)


def nt(a, b):
    return lax.dot_general(a, b, (((1,), (1,)), ((), ())), preferred_element_type=F32)


def tn(a, b):
    return lax.dot_general(a, b, (((0,), (0,)), ((), ())), preferred_element_type=F32)


def iota(shape, dim):
    return lax.broadcasted_iota(I32, shape, dim)


def onehot(mask):
    return jnp.where(mask, 1.0, 0.0).astype(BF)


def in_hbm(x):
    return pltpu.with_memory_space_constraint(x, pltpu.HBM)


def params(**kw):
    return pltpu.CompilerParams(vmem_limit_bytes=24 << 20, **kw)


def pack_kernel(assign_hbm, len_hbm, seq_ref, ids_hbm, inv_hbm, req_ref, pos_ref, *refs):
    msg_refs = refs[:4]
    assign_ref, len_ref, ids_ref, inv_ref, sems = refs[4:]
    loads = [
        pltpu.make_async_copy(src, dst, sems.at[k])
        for k, (src, dst) in enumerate(
            (
                (ids_hbm, ids_ref),
                (inv_hbm, inv_ref),
                (assign_hbm, assign_ref),
                (len_hbm, len_ref),
            )
        )
    ]
    for load in loads:
        load.start()
    loads[0].wait()
    ids = ids_ref[...]
    owner = ids >> 10
    local = (ids & (ROWS_DEV - 1)).astype(F32)
    held = iota((DEVICES, UNIQ), 0) == owner
    earlier = onehot(iota((UNIQ, UNIQ), 0) < iota((UNIQ, UNIQ), 1))
    before = nn(onehot(held), earlier)
    rank = jnp.sum(jnp.where(held, before, 0.0), axis=0, keepdims=True)
    pos_ref[...] = owner * 8 + rank.astype(I32)
    lane = iota((DEVICES, 4), 1)
    req = jnp.zeros((DEVICES, 4), F32)
    for r in range(4):
        chosen = held & (before == float(r))
        col = jnp.sum(jnp.where(chosen, ROWS_DEV - local, 0.0), axis=1, keepdims=True)
        req = jnp.where(lane == r, ROWS_DEV - col, req)
    req_ref[...] = req.astype(I32)
    for load in loads[1:]:
        load.wait()
    seq = seq_ref[0]
    for j in range(8):
        place = assign_ref[j]
        delta = (place // 8 - seq + 4) % 4
        half = place % 2
        row = jnp.concatenate(
            [inv_ref[j : j + 1, :], jnp.full((1, 128), len_ref[j], I32)], axis=1
        )
        for d in range(4):
            for b in range(2):

                @pl.when((delta == d) & (half == b))
                def _():
                    msg_refs[d][b : b + 1, :] = row


def pack(assignment, lengths, seq, ids, inverse):
    smem = pl.BlockSpec(memory_space=pltpu.SMEM)
    vmem = pl.BlockSpec(memory_space=pltpu.VMEM)
    hbm = pl.BlockSpec(memory_space=pltpu.HBM)
    return pl.pallas_call(
        pack_kernel,
        in_specs=[hbm, hbm, smem, hbm, hbm],
        scratch_shapes=[
            pltpu.SMEM((8,), I32),
            pltpu.SMEM((8,), I32),
            pltpu.VMEM((1, UNIQ), I32),
            pltpu.VMEM((8, MAXLEN), I32),
            pltpu.SemaphoreType.DMA((4,)),
        ],
        out_specs=[vmem] * 6,
        out_shape=[
            jax.ShapeDtypeStruct((DEVICES, 4), I32),
            jax.ShapeDtypeStruct((1, UNIQ), I32),
        ]
        + [jax.ShapeDtypeStruct((2, MAXLEN + 128), I32)] * 4,
        compiler_params=params(),
        name="pack",
    )(in_hbm(assignment), in_hbm(lengths), seq, in_hbm(ids.reshape(1, UNIQ)), in_hbm(inverse))


def tables_kernel(flipped_ref, pos_ref, win_hbm, wout_hbm, *refs):
    bias_ref, pos_rows_ref, winb_hbm, woutb_hbm, win_ref, wout_ref, winb_ref, woutb_ref, sems = refs
    loads = [
        pltpu.make_async_copy(win_hbm, win_ref, sems.at[0]),
        pltpu.make_async_copy(wout_hbm, wout_ref, sems.at[1]),
    ]
    stores = [
        pltpu.make_async_copy(winb_ref, winb_hbm, sems.at[2]),
        pltpu.make_async_copy(woutb_ref, woutb_hbm, sems.at[3]),
    ]
    for load in loads:
        load.start()
    i = iota((MAXLEN, MAXLEN), 0)
    j = iota((MAXLEN, MAXLEN), 1)
    for h in range(HEADS):
        line = jnp.broadcast_to(flipped_ref[h : h + 1, :], (MAXLEN, MAXLEN))
        spread = pltpu.roll(line, 1, 1, stride=1, stride_axis=0)
        full = jnp.where(j <= i, 0.5 * spread, MASKED)
        bias_ref[h] = full[:, :128]
    pos = jnp.broadcast_to(pos_ref[...], (UNIQ, UNIQ)).astype(F32)
    col = jnp.sum(jnp.where(i == j, pos, 0.0), axis=1, keepdims=True)
    pos_rows_ref[...] = jnp.broadcast_to(col.astype(I32), (UNIQ, 128))
    for load, store, src, dst in zip(loads, stores, (win_ref, wout_ref), (winb_ref, woutb_ref)):
        load.wait()
        for c in range(dst.shape[0]):
            dst[c] = src[:, pl.ds(c * 128, 128)]
        store.start()
    for store in stores:
        store.wait()


def tables(position_bias, pos, proj_in, proj_out):
    vmem = pl.BlockSpec(memory_space=pltpu.VMEM)
    hbm = pl.BlockSpec(memory_space=pltpu.HBM)
    return pl.pallas_call(
        tables_kernel,
        out_shape=[
            jax.ShapeDtypeStruct((HEADS, MAXLEN, 128), F32),
            jax.ShapeDtypeStruct((UNIQ, 128), I32),
            pltpu.HBM((16, D, 128), BF),
            pltpu.HBM((4, D, 128), BF),
        ],
        in_specs=[vmem, vmem, hbm, hbm],
        out_specs=[vmem, vmem, hbm, hbm],
        scratch_shapes=[
            pltpu.VMEM((D, 4 * D), BF),
            pltpu.VMEM((D, D), BF),
            pltpu.VMEM((16, D, 128), BF),
            pltpu.VMEM((4, D, 128), BF),
            pltpu.SemaphoreType.DMA((4,)),
        ],
        compiler_params=params(),
        name="tables",
    )(position_bias[:, ::-1], pos, in_hbm(proj_in), in_hbm(proj_out))


def asked_parts(asked_ref):
    asked = asked_ref[...]
    return (asked >> 5).astype(BF), (asked & 31).astype(BF)


def to_halves(x):
    groups = x.shape[0] // 8
    upper = iota((groups, 8, D // 2), 1) < 4
    low = x[:, : D // 2].reshape(groups, 8, D // 2)
    high = x[:, D // 2 :].reshape(groups, 8, D // 2)
    even = jnp.where(upper, low, pltpu.roll(high, 4, 1))
    odd = jnp.where(upper, pltpu.roll(low, 4, 1), high)
    both = jnp.concatenate([even[:, None], odd[:, None]], axis=1)
    return both.reshape(groups * 16, D // 2)


def from_halves(x):
    groups = x.shape[0] // 16
    upper = iota((groups, 8, D // 2), 1) < 4
    pairs = x.reshape(groups, 2, 8, D // 2)
    even = pairs[:, 0]
    odd = pairs[:, 1]
    low = jnp.where(upper, even, pltpu.roll(odd, 4, 1))
    high = jnp.where(upper, pltpu.roll(even, 4, 1), odd)
    flat = (groups * 8, D // 2)
    return jnp.concatenate([low.reshape(flat), high.reshape(flat)], axis=1)


def answer_kernel(asked_ref, table_hbm, out_hbm, table_ref, pick_ref, out_ref, sem):
    loads = []
    for c in range(4):
        part = pl.ds(c * 256, 256)
        loads.append(pltpu.make_async_copy(table_hbm.at[part], table_ref.at[part], sem.at[c]))
    for load in loads:
        load.start()
    high, low = asked_parts(asked_ref)
    count = 4 * DEVICES
    spread = onehot((iota((count, DEVICES), 0) >> 2) == iota((count, DEVICES), 1))
    value = nn(spread, high) * 32.0 + nn(spread, low)
    mine = iota((count, 4), 1) == (iota((count, 4), 0) & 3)
    col = jnp.sum(jnp.where(mine, value, 0.0), axis=1, keepdims=True).astype(I32)
    pick_ref[...] = onehot(iota((count, ROWS_DEV), 1) == col)
    for load in loads:
        load.wait()
    moves = []
    for c in range(2):
        rows = nn(pick_ref[pl.ds(c * 256, 256), :], table_ref[...])
        part = pl.ds(c * 512, 512)
        out_ref[part, :] = to_halves(rows).astype(BF)
        moves.append(pltpu.make_async_copy(out_ref.at[part], out_hbm.at[part], sem.at[4 + c]))
        moves[-1].start()
    for move in moves:
        move.wait()


def answer_rows(asked, table):
    return pl.pallas_call(
        answer_kernel,
        in_specs=[pl.BlockSpec(memory_space=pltpu.VMEM), pl.BlockSpec(memory_space=pltpu.HBM)],
        out_specs=pl.BlockSpec(memory_space=pltpu.HBM),
        out_shape=jax.ShapeDtypeStruct((8 * DEVICES, D // 2), BF),
        scratch_shapes=[
            pltpu.VMEM((ROWS_DEV, D), BF),
            pltpu.VMEM((4 * DEVICES, ROWS_DEV), BF),
            pltpu.VMEM((8 * DEVICES, D // 2), BF),
            pltpu.SemaphoreType.DMA((6,)),
        ],
        compiler_params=params(),
        name="answer",
    )(asked, in_hbm(table))


def compact_kernel(pos_ref, got_ref, out_ref):
    pos = pos_ref[:, :1]
    lane = iota((UNIQ, 8 * DEVICES), 1)
    for half in range(2):
        pick = onehot(lane == pos + 4 * half)
        out_ref[:, pl.ds(half * 256, 256)] = nn(pick, got_ref[...]).astype(BF)


def compact(pos_rows, got):
    return pl.pallas_call(
        compact_kernel,
        out_shape=jax.ShapeDtypeStruct((UNIQ, D), BF),
        compiler_params=params(),
        name="compact",
    )(pos_rows, got)


def row_mean(x):
    return jnp.sum(x, axis=-1, keepdims=True) * (1.0 / D)


def norm_parts(x):
    center = x - row_mean(x)
    spread = row_mean(center * center)
    inv = lax.rsqrt(spread + EPS)
    return center * inv, inv


def norm_grad(g, unit, inv):
    return inv * (g - row_mean(g) - unit * row_mean(g * unit))


def chunks(size, step=64):
    return [slice(r, r + step) for r in range(0, size, step)]


def side(ref, first, count, rs=slice(None)):
    return jnp.concatenate([ref[c, rs] for c in range(first, first + count)], axis=1)


def lay(ref, rs, value):
    for c in range(value.shape[1] // 128):
        ref[c, rs] = value[:, c * 128 : (c + 1) * 128].astype(BF)


ORDER = (6, 7, 4, 5, 2, 3, 0, 1)


def rows_body(long, one, two, counts, msg, rows, cot_ref, stage_ref, send, ready, acc_ref, fresh, refs):
    (win_ref, bin_ref, gin_ref, gmid_ref, wout_ref, bias_ref) = refs[:6]
    (hid, slope, wts, wslope, dpre, xs, unit_in, unit_mid, invs, narrow, wide) = refs[6:]
    size = MAXLEN
    every = slice(0, size)
    firsts, seconds = slice(0, 128), slice(128, 256)
    gin_half = 0.5 * gin_ref[...]
    start = jnp.where(long, 128, 0)
    lane = iota((1, 128), 1)
    ids_one, ids_two = msg
    line = jnp.concatenate(
        [
            jnp.where(lane < counts[0], ids_one[:, :128], -1),
            jnp.where(lane + start < counts[1], jnp.where(long, ids_one[:, 128:], ids_two[:, :128]), -1),
        ],
        axis=1,
    )
    cols = jnp.broadcast_to(line, (8, size)).astype(F32).T[:, :1].astype(I32)
    xs[...] = nn(onehot(iota((size, UNIQ), 1) == cols), rows)
    for rs in chunks(size):
        unit, inv = norm_parts(xs[rs])
        unit_in[rs] = unit
        invs[rs] = jnp.broadcast_to(inv, (rs.stop - rs.start, 128))
        lay(narrow, rs, unit * gin_half)
    for c in ORDER:
        ready(c)
        pre = nn(side(narrow, 0, 4, every), side(win_ref, 2 * c, 2))
        for k in range(2):
            blk = 2 * c + k
            half = pre[:, k * 128 : (k + 1) * 128] + 0.5 * bin_ref[:, pl.ds(blk * 128, 128)]
            up = 1.0 + jnp.tanh(half)
            act = (half * up).astype(BF)
            up = up.astype(BF)
            hid[blk] = act
            slope[blk] = up + act * (jnp.array(2.0, BF) - up)
    valid = [iota((128, 1), 0) < counts[0], iota((128, 1), 0) + start < counts[1]]
    per = []
    for part in range(2):
        inverse = 1.0 / jnp.full((1, 1), jnp.maximum(counts[part], 1), I32).astype(F32)
        per.append(jnp.where(valid[part], inverse, 0.0))
    cross = per[1] * jnp.where(long, 1.0, 0.0)
    blocks = ((0, 0, per[0]), (1, 1, per[1]), (1, 0, cross))
    cut = lambda i: slice(i * 128, i * 128 + 128)
    for h in range(HEADS):
        for bi, bj, scale in blocks:
            bias = bias_ref[h, (bi - bj) * 128 : (bi - bj) * 128 + 128, :]
            half = nt(hid[8 + h, cut(bi)], hid[12 + h, cut(bj)]) * (0.5 * SCALE) + bias
            up = 1.0 + jnp.tanh(half)
            act = half * up
            wts[h, bj, cut(bi)] = (act * scale).astype(BF)
            wslope[h, bj, cut(bi)] = ((up + act * (2.0 - up)) * (scale * (0.5 * SCALE))).astype(BF)
    for h in range(HEADS):
        for bi in range(2):
            wide[cut(bi), pl.ds(h * HEAD, HEAD)] = nn(
                side(wts.at[h], 0, bi + 1, cut(bi)), hid[4 + h, : (bi + 1) * 128]
            )
    for rs in chunks(size):
        unit, inv = norm_parts(wide[rs])
        unit_mid[rs] = unit
        lay(narrow, rs, unit * gmid_ref[...] * side(hid, 0, 4, rs).astype(F32))
        wide[rs, :128] = jnp.broadcast_to(inv, (rs.stop - rs.start, 128))
    ready(8)
    result = nn(side(narrow, 0, 4, every), side(wout_ref, 0, 4))
    other = jnp.where(long, one, two)
    for half, rs in enumerate((firsts, seconds)):
        stage_ref[rs] = jnp.where(valid[half], xs[rs] + result[rs], 0.0).astype(BF)
    send(one, 0, 0)
    send(other, pl.multiple_of(start, 128), 1)
    zero = jnp.zeros((), BF)
    lay(narrow, firsts, jnp.where(valid[0], cot_ref[one, :128, :], zero))
    lay(
        narrow,
        seconds,
        jnp.where(valid[1], cot_ref[other, pl.ds(pl.multiple_of(start, 128), 128), :], zero),
    )
    xs[...] = nt(side(narrow, 0, 4, every), side(wout_ref, 0, 4))
    for rs in chunks(size):
        unit = unit_mid[rs]
        inv = wide[rs, :1]
        grown = xs[rs] * gmid_ref[...]
        scaled = grown * unit
        for c in range(4):
            dpre[c, rs] = scaled[:, c * 128 : (c + 1) * 128].astype(BF) * slope[c, rs]
        lay(hid, rs, norm_grad(grown * side(hid, 0, 4, rs).astype(F32), unit, inv))
    for h in range(HEADS):
        for bi, bj, scale in blocks:
            ds = nt(hid[h, cut(bi)], hid[4 + h, cut(bj)]).astype(BF)
            wslope[h, bj, cut(bi)] = ds * wslope[h, bj, cut(bi)]
    for h in range(HEADS):
        for bi in range(2):
            dq = nn(side(wslope.at[h], 0, bi + 1, cut(bi)), hid[12 + h, : (bi + 1) * 128])
            dpre[8 + h, cut(bi)] = dq.astype(BF) * slope[8 + h, cut(bi)]
    for h in range(HEADS):
        for bj in range(2):
            qs = slice(bj * 128, size)
            dv = tn(wts[h, bj, qs], hid[h, qs])
            dpre[4 + h, cut(bj)] = dv.astype(BF) * slope[4 + h, cut(bj)]
            dk = tn(wslope[h, bj, qs], hid[8 + h, qs])
            dpre[12 + h, cut(bj)] = dk.astype(BF) * slope[12 + h, cut(bj)]
    wide[...] = nt(side(dpre, 0, 16, every), side(win_ref, 0, 16))
    for rs in chunks(size):
        dx = norm_grad(wide[rs] * gin_half, unit_in[rs], invs[rs, :1])
        lay(narrow, rs, dx + side(narrow, 0, 4, rs).astype(F32))
    sums = nn(onehot(iota((UNIQ, size), 0) == line), side(narrow, 0, 4, every))
    acc_ref[...] = jnp.where(fresh, sums, sums + acc_ref[...])


BOTH, EARLY, LATE = range(3)


def layer_kernel(plan, aliased, *refs):
    deltas, mode = plan
    n_src = len(deltas)
    refs = list(refs)
    info_ref = refs.pop(0)
    msgs = [refs.pop(0) for _ in range(n_src)]
    rows_refs = [refs.pop(0) for _ in range(n_src)]
    cot_ref = refs.pop(0)
    win_ref, bin_ref, gin_ref, gmid_ref, wout_ref, bias_ref = (refs.pop(0) for _ in range(6))
    if aliased:
        refs.pop(0)
    out_ref = refs.pop(0)
    part_refs = [refs.pop(0) for _ in range(n_src)]
    win_hbm, wout_hbm = win_ref, wout_ref
    if not aliased:
        win_ref, wout_ref = refs.pop(0), refs.pop(0)
    rows, ids_sc, acc, stages, blank, wsems, osems, zsems = (refs.pop(0) for _ in range(8))
    loads = {}
    if not aliased:
        for c in ORDER:
            part = pl.ds(2 * c, 2)
            loads[c] = pltpu.make_async_copy(win_hbm.at[part], win_ref.at[part], wsems.at[c])
        loads[8] = pltpu.make_async_copy(wout_hbm, wout_ref, wsems.at[8])
    for load in loads.values():
        load.start()
    work = (win_ref, bin_ref, gin_ref, gmid_ref, wout_ref, bias_ref, *refs)

    def ready(c):
        if c in loads:
            loads[c].wait()

    turns = 2 if mode == BOTH else 1
    steps = n_src * turns
    blank[...] = jnp.zeros((128, D), BF)

    def source(d):
        delta = jnp.int32(deltas[0])
        for k in range(1, n_src):
            delta = jnp.where(d == k, deltas[k], delta)
        lens = [info_ref[delta * 2 + b] for b in range(2)]
        base = ((info_ref[8] - delta + 4) % 4) * 2
        return base, lens, (lens[0] <= 128) & (lens[1] <= 128)

    def out_copy(t, place, start, half):
        return pltpu.make_async_copy(
            stages.at[t, pl.ds(half * 128, 128)],
            out_ref.at[place, pl.ds(start, 128)],
            osems.at[t, half],
        )

    def blank_copy(d, place, k):
        return pltpu.make_async_copy(
            blank, out_ref.at[place, pl.ds(128, 128)], zsems.at[d, k]
        )

    def step(t, carry):
        d = t // turns
        base, lens, short = source(d)
        long = jnp.logical_not(short)
        if mode == BOTH:
            turn = t % turns
            go = (turn == 0) | long
        elif mode == EARLY:
            turn = jnp.int32(0)
            go = long
        else:
            turn = jnp.where(short, 0, 1)
            go = None
        count = jnp.where(turn == 0, lens[0], lens[1])

        def work_on():
            for k in range(n_src):

                @pl.when(d == k)
                def _():
                    ids_sc[:2, :] = msgs[k][:, :MAXLEN]
                    rows[...] = rows_refs[k][...]

            if mode != EARLY:

                @pl.when(short)
                def _():
                    for k in range(2):
                        blank_copy(d, base + k, k).start()

            rows_body(
                long,
                base + turn,
                base + 1,
                (count, jnp.where(long, count, lens[1])),
                (ids_sc[pl.ds(turn, 1), :], ids_sc[1:2, :]),
                rows[...],
                cot_ref,
                stages.at[t],
                lambda place, start, half: out_copy(t, place, start, half).start(),
                ready,
                acc,
                (turn == 0) | (mode == LATE),
                work,
            )
            for k in range(n_src):

                @pl.when(d == k)
                def _():
                    part_refs[k][...] = acc[...].astype(BF)

        if mode == EARLY:

            @pl.when(short)
            def _():
                part_refs[0][...] = jnp.zeros((UNIQ, D), BF)
                for load in loads.values():
                    load.wait()

        if go is None:
            work_on()
        else:
            pl.when(go)(work_on)
        return carry

    if steps == 1:
        step(jnp.int32(0), 0)
    else:
        lax.fori_loop(0, steps, step, 0)
    for d in range(n_src):
        base, _, short = source(d)

        def sent(t):
            for half in range(2):
                out_copy(t, base, 0, half).wait()

        if mode == EARLY:
            pl.when(jnp.logical_not(short))(functools.partial(sent, 0))
        else:
            sent(d * turns)

            @pl.when(short)
            def _():
                for k in range(2):
                    blank_copy(d, base, k).wait()

            if mode == BOTH:
                pl.when(jnp.logical_not(short))(functools.partial(sent, d * turns + 1))


def layer(plan, info, msgs, rows, cot, weights, prior):
    deltas, mode = plan
    n_src = len(deltas)
    steps = n_src * (2 if mode == BOTH else 1)
    vmem = pl.BlockSpec(memory_space=pltpu.VMEM)
    hbm = pl.BlockSpec(memory_space=pltpu.HBM)
    args = [info, *msgs, *rows, cot, *weights]
    keep = [] if prior is not None else [weights[0], weights[4]]
    spec = vmem if prior is not None else hbm
    in_specs = [pl.BlockSpec(memory_space=pltpu.SMEM)] + [vmem] * (2 * n_src + 1)
    in_specs += [spec, vmem, vmem, vmem, spec, vmem]
    alias = {}
    if prior is not None:
        alias = {len(args): 0}
        args.append(prior)
        in_specs.append(hbm)
    part = jax.ShapeDtypeStruct((UNIQ, D), BF)
    dma = pltpu.SemaphoreType.DMA
    return pl.pallas_call(
        functools.partial(layer_kernel, plan, prior is not None),
        in_specs=in_specs,
        out_specs=[hbm] + [vmem] * (n_src + len(keep)),
        scratch_shapes=[
            pltpu.VMEM((UNIQ, D), BF),
            pltpu.VMEM((8, MAXLEN), I32),
            pltpu.VMEM((UNIQ, D), F32),
            pltpu.VMEM((steps, MAXLEN, D), BF),
            pltpu.VMEM((128, D), BF),
            dma((9,)),
            dma((steps, 2)),
            dma((n_src, 2)),
            pltpu.VMEM((16, MAXLEN, 128), BF),
            pltpu.VMEM((16, MAXLEN, 128), BF),
            pltpu.VMEM((HEADS, 2, MAXLEN, 128), BF),
            pltpu.VMEM((HEADS, 2, MAXLEN, 128), BF),
            pltpu.VMEM((16, MAXLEN, 128), BF),
            pltpu.VMEM((MAXLEN, D), F32),
            pltpu.VMEM((MAXLEN, D), F32),
            pltpu.VMEM((MAXLEN, D), F32),
            pltpu.VMEM((MAXLEN, 128), F32),
            pltpu.VMEM((4, MAXLEN, 128), BF),
            pltpu.VMEM((MAXLEN, D), F32),
        ],
        out_shape=[jax.ShapeDtypeStruct(cot.shape, BF)]
        + [part] * n_src
        + [jax.ShapeDtypeStruct(w.shape, BF) for w in keep],
        input_output_aliases=alias,
        compiler_params=params(),
        name="layer",
    )(*args)


def info_kernel(seq_ref, *refs):
    out_ref = refs[-1]
    for d in range(4):
        for b in range(2):
            out_ref[2 * d + b] = refs[d][b, MAXLEN]
    out_ref[8] = seq_ref[0]


def scalars(seq, msgs):
    smem = pl.BlockSpec(memory_space=pltpu.SMEM)
    return pl.pallas_call(
        info_kernel,
        in_specs=[smem] * 5,
        out_specs=smem,
        out_shape=jax.ShapeDtypeStruct((16,), I32),
        compiler_params=params(),
        name="scalars",
    )(seq, *msgs)


def expand_kernel(pos_ref, *refs):
    out_hbm, out_ref, sems = refs[-3:]
    total = refs[0][...].astype(F32)
    for r in refs[1:-3]:
        total = total + r[...].astype(F32)
    total = total.astype(BF)
    pos = pos_ref[...]
    size = 256
    moves = []
    for c in range(8 * DEVICES // size):
        row = iota((size, UNIQ), 0) + c * size
        upper = nn(onehot(row == pos), total[:, : D // 2])
        lower = nn(onehot(row == pos + 4), total[:, D // 2 :])
        part = pl.ds(c * size, size)
        out_ref[part, :] = (upper + lower).astype(BF)
        moves.append(pltpu.make_async_copy(out_ref.at[part], out_hbm.at[part], sems.at[c]))
        moves[-1].start()
    for move in moves:
        move.wait()


def expand(pos, parts):
    vmem = pl.BlockSpec(memory_space=pltpu.VMEM)
    return pl.pallas_call(
        expand_kernel,
        in_specs=[vmem] * (1 + len(parts)),
        out_specs=pl.BlockSpec(memory_space=pltpu.HBM),
        out_shape=jax.ShapeDtypeStruct((8 * DEVICES, D // 2), BF),
        scratch_shapes=[
            pltpu.VMEM((8 * DEVICES, D // 2), BF),
            pltpu.SemaphoreType.DMA((4,)),
        ],
        compiler_params=params(),
        name="expand",
    )(pos, *parts)


def asked_line_kernel(asked_ref, out_ref):
    parts = []
    shape = (DEVICES, 4 * DEVICES)
    spread = onehot(iota(shape, 0) == (iota(shape, 1) >> 2))
    for part in asked_parts(asked_ref):
        square = jnp.concatenate([part.astype(F32), jnp.zeros((DEVICES, 124), F32)], axis=1)
        parts.append(nn(square.T[:8].astype(BF), spread))
    value = parts[0] * 32.0 + parts[1]
    mine = iota((8, 4 * DEVICES), 0) == (iota((8, 4 * DEVICES), 1) & 3)
    out_ref[...] = jnp.sum(jnp.where(mine, value, 0.0), axis=0, keepdims=True).astype(I32)


def asked_line(asked):
    return pl.pallas_call(
        asked_line_kernel,
        out_shape=jax.ShapeDtypeStruct((1, 4 * DEVICES), I32),
        compiler_params=params(),
        name="asked_line",
    )(asked)


def scatter_kernel(line_ref, landed_ref, out_hbm, whole_ref, rows_ref, sems):
    whole_ref[...] = from_halves(landed_ref[...].astype(F32)).astype(BF)
    size = 256
    moves = []
    for c in range(ROWS_DEV // size):
        row = iota((size, 4 * DEVICES), 0) + c * size
        rows_ref[pl.ds(c * size, size), :] = nn(onehot(row == line_ref[...]), whole_ref[...])
        for k in range(2):
            part = pl.ds(c * size + k * 128, 128)
            move = pltpu.make_async_copy(rows_ref.at[part], out_hbm.at[part], sems.at[2 * c + k])
            move.start()
            moves.append(move)
    for move in moves:
        move.wait()


def scatter(line, landed):
    vmem = pl.BlockSpec(memory_space=pltpu.VMEM)
    return pl.pallas_call(
        scatter_kernel,
        in_specs=[vmem, vmem],
        out_specs=pl.BlockSpec(memory_space=pltpu.HBM),
        out_shape=jax.ShapeDtypeStruct((ROWS_DEV, D), F32),
        scratch_shapes=[
            pltpu.VMEM((4 * DEVICES, D), BF),
            pltpu.VMEM((ROWS_DEV, D), F32),
            pltpu.SemaphoreType.DMA((8,)),
        ],
        compiler_params=params(),
        name="scatter",
    )(line, landed)


def ring(delta):
    return [(i, (i + delta) % 4) for i in range(4)]


def exchange(x, shape):
    got = lax.all_to_all(x.reshape(shape), ("emb", "seq"), split_axis=0, concat_axis=0, tiled=True)
    return got.reshape(x.shape)


PLANS = (((0,), EARLY), ((1,), BOTH), ((3, 2), BOTH), ((0,), LATE))


def program(
    item_table,
    unique_ids,
    inverse,
    lengths,
    assignment,
    proj_in,
    bias_in,
    gain_in,
    gain_mid,
    proj_out,
    position_bias,
    cotangent,
):
    seq = lax.axis_index("seq").astype(I32).reshape(1)
    req, pos, *sent = pack(assignment, lengths, seq, unique_ids, inverse)
    asked = exchange(req, (DEVICES, 1, 4))
    msgs = [sent[0]] + [lax.ppermute(sent[d], "seq", ring(d)) for d in (1, 2, 3)]
    bias, pos_rows, win, wout = tables(position_bias, pos, proj_in, proj_out)
    answer = answer_rows(asked, item_table)
    got = exchange(answer, (DEVICES, 8, D // 2))
    info = scalars(seq, msgs)
    got, info = lax.optimization_barrier((got, info))
    line = asked_line(asked)
    own = compact(pos_rows, got)
    rows = [own]
    for d in (1, 2, 3):
        rows.append(lax.ppermute(own, "seq", ring(d)))
    weights = (
        in_hbm(win),
        bias_in.reshape(1, 4 * D),
        gain_in.reshape(1, D),
        gain_mid.reshape(1, D),
        in_hbm(wout),
        bias,
    )
    outputs = None
    sums = []
    for plan in PLANS:
        outputs, *parts = layer(
            plan,
            info,
            [msgs[d] for d in plan[0]],
            [rows[d] for d in plan[0]],
            cotangent,
            weights,
            outputs,
        )
        if len(parts) > len(plan[0]):
            weights = (parts[-2], *weights[1:4], parts[-1], weights[5])
        for d, part in zip(plan[0], parts):
            sums.append(part if d == 0 else lax.ppermute(part, "seq", ring(-d)))
    landed = exchange(expand(pos, sums), (DEVICES, 8, D // 2))
    return (outputs, scatter(line, landed))


def solution(mesh):
    both = ("emb", "seq")
    in_specs = (
        P(both, None),
        P(both),
        P(both, None),
        P(both),
        P(both),
        P(),
        P(),
        P(),
        P(),
        P(),
        P(),
        P(both, None, None),
    )
    out_specs = (P(both, None, None), P(both, None))
    return jax.shard_map(program, mesh=mesh, in_specs=in_specs, out_specs=out_specs, check_vma=False)
```
